256 devices in a mesh: samp: 8 (over z), feat: 32 (over y, x, core).
Axes of the slice: x: 4, y: 4, z: 8, core: 2. Of those that a mesh axis runs over, the one named last changes fastest.
Arguments:
- data: bfloat16 [32768, 512], P('samp'), may hold values from -6 to 6
- omega: bfloat16 [512, 24576], P(None, 'feat'), may hold values from -0.25 to 0.25
- phase: float32 [24576], P('feat'), may hold values from -3.140625 to 3.140625
- earlier: bfloat16 [24576, 12288], P('feat', 'samp'), may hold values from -3 to 3, as said below
- ridge: float32 [1], replicated, may hold values from 0.5 to 2
Outputs:
- factor: float32 [24576, 512], P('feat')
The draws below stay inside these ranges and needn't reach their ends.
Inputs may be any that keep to these rules, and one draw needn't show every extreme that they name: The spectral norm of earlier[:512] is at most 0.56, so that shifted[:512] is positive definite.
All inputs are finite; a program needn't handle non-finite values.
Results may differ from the reference program's by a relative error of at most 0.015.
Values may be sent and summed in bfloat16 or wider, within the bound.
No kernel may reach another device: no remote copies, remote signals or barrier semaphores. Data moves between devices by JAX's collectives and lax.ppermute only.
A program may use at most 128 MiB of HBM per device.

```python
import math
import jax
import jax.numpy as jnp
from jax import lax

DIN = 512
PANEL = 512
TRAIL = 24576
EARLIER = 12288
SAMPLES = 32768


def draw_earlier(key, part):
    base = jax.random.fold_in(key, 7331)
    key_basis, key_signs, key_rows, key_scale, key_spread, key_trail = jax.random.split(base, 6)
    frequency = (jax.random.permutation(key_basis, EARLIER - 1)[:PANEL] + 1).astype(jnp.int32)
    columns = jnp.arange(EARLIER, dtype=jnp.int32)
    angle_steps = frequency[:, None] * (2 * columns[None, :] + 1) % (4 * EARLIER)
    column_sign = (2 * jax.random.randint(key_signs, (EARLIER,), 0, 2) - 1).astype(jnp.float32)
    row_basis = jnp.sqrt(jnp.float32(2.0) / EARLIER) * jnp.cos(jnp.float32(math.pi) * angle_steps.astype(jnp.float32) / (2.0 * EARLIER)) * column_sign[None, :]
    position = jnp.arange(PANEL, dtype=jnp.int32)
    mix_steps = position[:, None] * (2 * position[None, :] + 1) % (4 * PANEL)
    norming = jnp.where(position[:, None] == 0, jnp.sqrt(jnp.float32(1.0) / PANEL), jnp.sqrt(jnp.float32(2.0) / PANEL))
    cosine_mix = norming * jnp.cos(jnp.float32(math.pi) * mix_steps.astype(jnp.float32) / (2.0 * PANEL))
    row_sign = (2 * jax.random.randint(key_rows, (PANEL,), 0, 2) - 1).astype(jnp.float32)
    row_scale = jax.random.uniform(key_scale, (PANEL,), jnp.float32, 0.3, 0.55)
    column_scale = jax.random.uniform(key_spread, (PANEL,), jnp.float32, 0.35, 1.0)
    mixing = (row_scale * row_sign)[:, None] * cosine_mix * column_scale[None, :]
    panel_rows = jnp.dot(mixing, row_basis, precision=lax.Precision.HIGHEST)
    trailing_rows = 0.5 * jax.random.truncated_normal(key_trail, -6.0, 6.0, (TRAIL - PANEL, EARLIER), jnp.float32)
    return jnp.concatenate([panel_rows, trailing_rows], axis=0).astype(jnp.bfloat16)


def block_scale(key, extent, cuts, low, high):
    loudness = 1.0
    for dim, shards_of in cuts:
        draws = jax.random.uniform(jax.random.fold_in(jax.random.fold_in(key, 6), dim), (shards_of,), jnp.float32, low / len(cuts), high / len(cuts))
        loudness = loudness * jnp.repeat(jnp.exp(draws), extent[dim] // shards_of).reshape((-1,) + (1,) * (len(extent) - 1 - dim))
    return loudness


def scatter_about(stream_key, extent, width, most, cuts=(), kind=jnp.bfloat16):
    entries = jax.random.normal(stream_key, extent, jnp.float32) * width
    if len(cuts) > 0:
        entries = block_scale(stream_key, extent, cuts, -0.22, 0.18) * entries
    return jnp.clip(entries, min=-most, max=most).astype(kind)


def setup_inputs(seed: int = 0) -> dict:
    seeds = jax.random.split(jax.random.key(seed), 6)
    return {
        "data": scatter_about(seeds[0], (SAMPLES, DIN), 1.0, 6.0, ((0, 8),)),
        "omega": scatter_about(seeds[1], (DIN, TRAIL), DIN ** -0.5, 0.25, ((1, 32),)),
        "phase": jnp.clip(jax.random.uniform(seeds[2], (TRAIL,), jnp.float32, -3.140625, 3.140625), -3.140625, 3.140625),
        "earlier": draw_earlier(jax.random.fold_in(seeds[5], 71), 0),
        "ridge": jnp.clip(jnp.exp(jax.random.uniform(seeds[4], (1,), jnp.float32, math.log(0.5), math.log(2.0))), 0.5, 2.0),
    }


def reference(data, omega, phase, earlier, ridge):
    scale = jnp.sqrt(jnp.float32(2.0) / SAMPLES)

    def features(weights, shift):
        proj = jnp.dot(data.astype(jnp.float32), weights.astype(jnp.float32), preferred_element_type=jnp.float32) + shift[None, :]
        return (scale * jnp.cos(proj)).astype(jnp.bfloat16)
    panel_feat = features(omega[:, :PANEL], phase[:PANEL])

    def block_gram(index):
        start = (index * PANEL).astype(jnp.int32)
        weights = lax.dynamic_slice_in_dim(omega, start, PANEL, 1)
        shift = lax.dynamic_slice_in_dim(phase, start, PANEL, 0)
        block = features(weights, shift)
        return lax.dot_general(block.astype(jnp.float32), panel_feat.astype(jnp.float32), (((0,), (0,)), ((), ())), preferred_element_type=jnp.float32)
    gram = lax.map(block_gram, jnp.arange(TRAIL // PANEL, dtype=jnp.int32)).reshape(TRAIL, PANEL)
    update = lax.dot_general(earlier.astype(jnp.float32), earlier[:PANEL].astype(jnp.float32), (((1,), (1,)), ((), ())), preferred_element_type=jnp.float32)
    row_ids = jnp.arange(TRAIL, dtype=jnp.int32)
    col_ids = jnp.arange(PANEL, dtype=jnp.int32)
    shifted = gram - update + ridge[0] * (row_ids[:, None] == col_ids[None, :]).astype(jnp.float32)
    lower = jnp.linalg.cholesky(shifted[:PANEL])
    return lax.linalg.triangular_solve(lower, shifted, left_side=False, lower=True, transpose_a=True)
```

```python
import functools
import math

import jax
import jax.numpy as jnp
import numpy as np
from jax import lax
from jax.experimental import pallas as pl
from jax.experimental.pallas import tpu as pltpu
from jax.sharding import PartitionSpec as P

PANEL = 512
SIDE = 4
EXTRA = 16
HIGHEST = lax.Precision.HIGHEST
NT = (((1,), (1,)), ((), ()))
TN = (((0,), (0,)), ((), ()))
INV_TURN = 1.0 / (2.0 * math.pi)
MAGIC = 12582912.0


def sine_coefficients():
    u = np.cos(np.pi * (np.arange(4000) + 0.5) / 4000) * 0.25
    fit = np.polynomial.chebyshev.Chebyshev.fit(u * u, -np.sin(2 * np.pi * u) / u, 4, domain=[0, 1 / 16])
    poly = fit.convert(kind=np.polynomial.Polynomial, domain=[-1, 1], window=[-1, 1])
    return [float(v) for v in poly.coef]


SINE = sine_coefficients()


def scaled_cos(turns, scale):
    r = turns - ((turns + MAGIC) - MAGIC)
    u = jnp.abs(r) - 0.25
    s = u * u
    coefs = [v * scale for v in SINE]
    p = coefs[4]
    for v in coefs[3::-1]:
        p = p * s + v
    return p * u


def local_kernel(w_ref, ph_ref, x_ref, o_ref, *, scale):
    proj = lax.dot_general(w_ref[...], x_ref[...], NT, preferred_element_type=jnp.float32)
    o_ref[...] = scaled_cos(proj * INV_TURN + ph_ref[...], scale).astype(jnp.bfloat16)


def local_features(wt, ph, data, scale, bs=1024):
    rows, din = wt.shape
    samples = data.shape[0]
    return pl.pallas_call(
        functools.partial(local_kernel, scale=scale),
        grid=(samples // bs,),
        in_specs=[
            pl.BlockSpec((rows, din), lambda i: (0, 0)),
            pl.BlockSpec((rows, 1), lambda i: (0, 0)),
            pl.BlockSpec((bs, din), lambda i: (i, 0)),
        ],
        out_specs=pl.BlockSpec((rows, bs), lambda i: (0, i)),
        out_shape=jax.ShapeDtypeStruct((rows, samples), jnp.bfloat16),
        cost_estimate=pl.CostEstimate(flops=2 * rows * samples * din, bytes_accessed=12 << 20, transcendentals=0),
        name="local_features",
    )(wt, ph, data)


def gram_kernel(pos_ref, v_ref, x_ref, f_ref, e_ref, s_ref, d_ref, ph_ref, phd_ref, *, scale):
    i = pl.program_id(0)
    y, x, c, row = pos_ref[0], pos_ref[1], pos_ref[2], pos_ref[3]

    def piece(p):
        half, q = p // SIDE, p % SIDE
        return (c, lax.rem(x - q + SIDE, SIDE)) if half == 0 else (1 - c, lax.rem(y - q + SIDE, SIDE))

    def rows_of(p):
        a, b = piece(p)
        return v_ref[a, b, :256, :]

    def row_slice(p):
        a, b = piece(p)
        return v_ref[a, b, pl.ds(pl.multiple_of(lax.rem(row, 256), 16), 16), :]

    def sixteen(p):
        return jnp.where(row < 256, row_slice(p).astype(jnp.float32), row_slice(p + 1).astype(jnp.float32)).astype(jnp.bfloat16)

    @pl.when(i == 0)
    def _():
        a, b = piece(0)
        tail = v_ref[a, b, 256:256 + EXTRA, :].astype(jnp.float32)
        ph = (tail[0:1] + tail[1:2]) + tail[2:3]
        ph_ref[...] = ph
        hit = lax.broadcasted_iota(jnp.int32, (16, PANEL), 1) == row + lax.broadcasted_iota(jnp.int32, (16, PANEL), 0)
        phd_ref[...] = jnp.sum(jnp.where(hit, jnp.broadcast_to(ph, (16, PANEL)), 0.0), axis=1, keepdims=True)
        s_ref[...] = jnp.zeros_like(s_ref)
        d_ref[...] = jnp.zeros_like(d_ref)

    for chunk in range(3):
        @pl.when(i == chunk)
        def _(chunk=chunk):
            for h in range(2):
                panel = rows_of(2 + 2 * chunk + h)
                cols = slice(256 * h, 256 * h + 256)
                s_ref[:, cols] -= lax.dot_general(e_ref[...], panel, NT, preferred_element_type=jnp.float32)
                d_ref[:, cols] -= lax.dot_general(sixteen(2 + 2 * chunk), panel, NT, preferred_element_type=jnp.float32)

    data = x_ref[...]
    panel_feat = []
    for h in range(2):
        proj = lax.dot_general(data, rows_of(h), NT, preferred_element_type=jnp.float32)
        panel_feat.append(scaled_cos(proj * INV_TURN + ph_ref[:, 256 * h:256 * h + 256], scale).astype(jnp.bfloat16))
    proj = lax.dot_general(sixteen(0), data, NT, preferred_element_type=jnp.float32)
    feat = scaled_cos(proj * INV_TURN + phd_ref[...], scale).astype(jnp.bfloat16)
    for h in range(2):
        cols = slice(256 * h, 256 * h + 256)
        s_ref[:, cols] += jnp.dot(f_ref[...], panel_feat[h], preferred_element_type=jnp.float32)
        d_ref[:, cols] += jnp.dot(feat, panel_feat[h], preferred_element_type=jnp.float32)


def gram(pos, v, data, feat, earlier, scale, bs=512):
    rows, samples = feat.shape
    din = data.shape[1]
    return pl.pallas_call(
        functools.partial(gram_kernel, scale=scale),
        grid=(samples // bs,),
        in_specs=[
            pl.BlockSpec(memory_space=pltpu.SMEM),
            pl.BlockSpec(v.shape, lambda i: (0, 0, 0, 0)),
            pl.BlockSpec((bs, din), lambda i: (i, 0)),
            pl.BlockSpec((rows, bs), lambda i: (0, i)),
            pl.BlockSpec((rows, PANEL), lambda i: (0, jnp.minimum(i, 2))),
        ],
        out_specs=[pl.BlockSpec((rows, PANEL), lambda i: (0, 0)), pl.BlockSpec((16, PANEL), lambda i: (0, 0))],
        out_shape=[
            jax.ShapeDtypeStruct((rows, PANEL), jnp.float32),
            jax.ShapeDtypeStruct((16, PANEL), jnp.float32),
        ],
        scratch_shapes=[pltpu.VMEM((1, PANEL), jnp.float32), pltpu.VMEM((16, 1), jnp.float32)],
        cost_estimate=pl.CostEstimate(flops=8 << 30, bytes_accessed=16 << 20, transcendentals=0),
        name="gram",
    )(pos, v, data, feat, earlier)


def split2(v):
    high = v.astype(jnp.bfloat16)
    return high, (v - high.astype(jnp.float32)).astype(jnp.bfloat16)


def split3(v):
    high = v.astype(jnp.bfloat16)
    rest = v - high.astype(jnp.float32)
    mid = rest.astype(jnp.bfloat16)
    return high, mid, (rest - mid.astype(jnp.float32)).astype(jnp.bfloat16)


def block_inverse(n_ref, lb_ref):
    sub = lax.broadcasted_iota(jnp.int32, (8, 128), 0)
    lane = lax.broadcasted_iota(jnp.int32, (8, 128), 1)

    def step(s, carry):
        k = pl.multiple_of(s * 8, 8)
        rows = n_ref[pl.ds(k, 8), :]
        pivot = pltpu.roll(rows[:, :128], jnp.where(s == 0, 0, 128 - k), 1)
        a = [[None] * 8 for _ in range(8)]
        for j in range(8):
            col = jnp.broadcast_to(pivot[:, j:j + 1], (8, 128))
            for i in range(j, 8):
                a[i][j] = jnp.broadcast_to(col[i:i + 1, :], (8, 128))
        low = [[None] * 8 for _ in range(8)]
        root = []
        for j in range(8):
            inverse = 1.0 / a[j][j]
            root.append(lax.rsqrt(a[j][j]))
            for i in range(j + 1, 8):
                low[i][j] = a[i][j] * inverse
            for i in range(j + 1, 8):
                for m in range(j + 1, i + 1):
                    a[i][m] = a[i][m] - low[i][j] * a[m][j]
        t = [[None] * 8 for _ in range(8)]
        for j in range(8):
            for i in range(j + 1, 8):
                acc = low[i][j]
                for m in range(j + 1, i):
                    acc = acc + low[i][m] * t[m][j]
                t[i][j] = -acc
        w0 = jnp.zeros((8, 128), jnp.float32)
        w1 = jnp.zeros((8, 128), jnp.float32)
        for j in range(8):
            col = jnp.where(sub == j, root[j], 0.0)
            for i in range(j + 1, 8):
                col = jnp.where(sub == i, root[i] * t[i][j], col)
            w0 = w0 + col * jnp.broadcast_to(rows[j:j + 1, :128], (8, 128))
            w1 = w1 + col * jnp.broadcast_to(rows[j:j + 1, 128:], (8, 128))
        lb_ref[pl.ds(k, 8), :] = w1
        gh, gm, gl = split3(jnp.where(lane >= k + 8, w0, 0.0))
        wh, wm, wl = split3(jnp.concatenate([w0, w1], axis=1))
        left = jnp.concatenate([gh, gh, gm, gh, gm, gl], axis=0)
        right = jnp.concatenate([wh, wm, wh, wl, wm, wh], axis=0)
        n_ref[...] -= lax.dot_general(left, right, TN, preferred_element_type=jnp.float32)
        return carry

    lax.fori_loop(0, 16, step, 0)


def factor_kernel(ridge_ref, d_ref, out_ref, m_ref, j_ref, n_ref, lb_ref):
    n = PANEL
    eye = lax.broadcasted_iota(jnp.int32, (n, n), 0) == lax.broadcasted_iota(jnp.int32, (n, n), 1)
    m_ref[...] = d_ref[...].reshape(n, n) + jnp.where(eye, ridge_ref[0], 0.0)
    j_ref[...] = jnp.where(eye, 1.0, 0.0)
    out_ref[...] = jnp.zeros((n, n), jnp.float32)
    small = lax.broadcasted_iota(jnp.int32, (128, 128), 0) == lax.broadcasted_iota(jnp.int32, (128, 128), 1)
    for b in range(n // 128):
        r0, r1 = 128 * b, 128 * b + 128
        n_ref[:, :128] = m_ref[r0:r1, r0:r1]
        n_ref[:, 128:] = jnp.where(small, 1.0, 0.0)
        block_inverse(n_ref, lb_ref)
        lb = lb_ref[...]
        jb = jnp.dot(lb, j_ref[r0:r1, :r1], precision=HIGHEST, preferred_element_type=jnp.float32)
        out_ref[r0:r1, :r1] = jb
        if r1 < n:
            r = jnp.dot(lb, m_ref[r0:r1, r1:], precision=HIGHEST, preferred_element_type=jnp.float32)
            m_ref[r1:, r1:] -= lax.dot_general(r, r, TN, precision=HIGHEST, preferred_element_type=jnp.float32)
            j_ref[r1:, :r1] -= lax.dot_general(r, jb, TN, precision=HIGHEST, preferred_element_type=jnp.float32)


def factor_inverse(ridge, d):
    n = PANEL
    return pl.pallas_call(
        factor_kernel,
        out_shape=jax.ShapeDtypeStruct((n, n), jnp.float32),
        in_specs=[pl.BlockSpec(memory_space=pltpu.SMEM), pl.BlockSpec(memory_space=pltpu.VMEM)],
        out_specs=pl.BlockSpec(memory_space=pltpu.VMEM),
        scratch_shapes=[
            pltpu.VMEM((n, n), jnp.float32),
            pltpu.VMEM((n, n), jnp.float32),
            pltpu.VMEM((128, 256), jnp.float32),
            pltpu.VMEM((128, 128), jnp.float32),
        ],
        cost_estimate=pl.CostEstimate(flops=8 << 30, bytes_accessed=2 << 20, transcendentals=0),
        name="factor_inverse",
    )(ridge, d)


def solve_kernel(pos_ref, ridge_ref, s_ref, inv_ref, o_ref):
    rows = s_ref.shape[0]
    row_ids = pos_ref[4] + lax.broadcasted_iota(jnp.int32, (rows, PANEL), 0)
    hit = row_ids == lax.broadcasted_iota(jnp.int32, (rows, PANEL), 1)
    sh, sl = split2(s_ref[...] + jnp.where(hit, ridge_ref[0], 0.0))
    for b in range(PANEL // 256):
        r0, r1 = 256 * b, 256 * b + 256
        lh, ll = split2(inv_ref[r0:r1, :r1])
        out = lax.dot_general(sh[:, :r1], ll, NT, preferred_element_type=jnp.float32)
        out += lax.dot_general(sl[:, :r1], lh, NT, preferred_element_type=jnp.float32)
        o_ref[:, r0:r1] = out + lax.dot_general(sh[:, :r1], lh, NT, preferred_element_type=jnp.float32)


def solve(pos, ridge, s, inverse, bs=256):
    rows = s.shape[0]
    smem = pl.BlockSpec(memory_space=pltpu.SMEM)
    return pl.pallas_call(
        solve_kernel,
        out_shape=jax.ShapeDtypeStruct(s.shape, jnp.float32),
        in_specs=[smem, smem, pl.BlockSpec(memory_space=pltpu.VMEM), pl.BlockSpec(memory_space=pltpu.VMEM)],
        out_specs=pl.BlockSpec(memory_space=pltpu.VMEM),
        cost_estimate=pl.CostEstimate(flops=6 * rows * PANEL * PANEL, bytes_accessed=4 << 20, transcendentals=0),
        name="solve",
    )(pos, ridge, s, inverse)


def feat_of(y, x, c):
    return ((y % SIDE) * SIDE + x % SIDE) * 2 + c


def share_panel(mine, partner, y, x, c):
    side = range(SIDE)

    def permute(value, pairs):
        return lax.ppermute(value, "feat", pairs)

    def first(value, received, has):
        total = received[0] + received[1] + received[2]
        return jnp.where(has, value, total)

    half = permute(partner, [(feat_of(0, 0, 0), feat_of(0, 0, 1))])
    half = jnp.where(c == 0, mine, half)
    got = [permute(half[k], [(feat_of(0, 0, 0), feat_of(0, k, 0)), (feat_of(0, 0, 1), feat_of(k, 0, 1))]) for k in (1, 2, 3)]
    held = first(half[0], got, (x == 0) & (y == 0))
    got = [
        permute(
            held,
            [(feat_of(0, j, 0), feat_of(k, j, 0)) for j in side] + [(feat_of(j, 0, 1), feat_of(j, k, 1)) for j in side],
        )
        for k in (1, 2, 3)
    ]
    held = first(held, got, jnp.where(c == 0, y, x) == 0)
    got = [
        permute(
            held,
            [(feat_of(i, j, 0), feat_of(i, j + k, 0)) for i in side for j in side]
            + [(feat_of(i, j, 1), feat_of(i + k, j, 1)) for i in side for j in side],
        )
        for k in (1, 2, 3)
    ]
    own = jnp.stack([held, *got])
    other = permute(own, [(i, i ^ 1) for i in range(2 * SIDE * SIDE)])
    return jnp.stack([own, other])


def on_device(data, omega, phase, earlier, ridge):
    samples_all = data.shape[0] * lax.axis_size("samp")
    scale = math.sqrt(2.0 / samples_all)
    feat = lax.axis_index("feat")
    rows = omega.shape[1]
    c = feat % 2
    x = (feat // 2) % SIDE
    y = feat // (2 * SIDE)
    pos = jnp.stack([y, x, c, feat * 16, feat * rows]).astype(jnp.int32)

    weights = omega.T
    turns = phase * INV_TURN
    high = lax.reduce_precision(turns, 8, 7)
    mid = lax.reduce_precision(turns - high, 8, 7)
    low = turns - high - mid
    tail = jnp.stack([high[:PANEL], mid[:PANEL], low[:PANEL]]).astype(jnp.bfloat16)
    tail = jnp.concatenate([tail, jnp.zeros((EXTRA - 3, PANEL), jnp.bfloat16)])

    def with_tail(blocks):
        return jnp.stack([jnp.concatenate([b, tail]) for b in blocks])

    def panel_rows(k):
        return [earlier[256 * h:256 * h + 256, PANEL * k:PANEL * k + PANEL] for h in range(2)]

    mine = with_tail([weights[:256], weights[256:512], *panel_rows(0)])
    partner = with_tail([*panel_rows(1), *panel_rows(2)])
    v = share_panel(mine, partner, y, x, c)

    local = local_features(weights, turns[:, None], data, scale)
    s, d = gram(pos, v, data, local, earlier, scale)
    summed = lax.psum(s, "samp")
    d = lax.all_to_all(jnp.broadcast_to(d, (8, 16, PANEL)), "samp", 0, 0).sum(0)
    d = lax.all_to_all(jnp.broadcast_to(d, (32, 16, PANEL)), "feat", 0, 0)
    inverse = factor_inverse(ridge, d)
    return solve(pos, ridge, summed, inverse)


def solution(mesh):
    in_specs = (P("samp", None), P(None, "feat"), P("feat"), P("feat", "samp"), P())
    out_specs = P("feat", None)
    return jax.shard_map(
        on_device, mesh=mesh, in_specs=in_specs, out_specs=out_specs, check_vma=False
    )
```

```python
import functools
import math

import jax
import jax.numpy as jnp
import numpy as np
from jax import lax
from jax.experimental import pallas as pl
from jax.experimental.pallas import tpu as pltpu
from jax.sharding import PartitionSpec as P


PANEL = 512
SIDE = 4
SAMPLE_BLOCK = 512
EXTRA = 16
HIGHEST = lax.Precision.HIGHEST
NT = (((1,), (1,)), ((), ()))
TN = (((0,), (0,)), ((), ()))
INV_TURN = 1.0 / (2.0 * math.pi)
DEGREE = 4
MAGIC = 12582912.0


def sine_coefficients():
    u = np.cos(np.pi * (np.arange(4000) + 0.5) / 4000) * 0.25
    fit = np.polynomial.chebyshev.Chebyshev.fit(u * u, -np.sin(2 * np.pi * u) / u, DEGREE, domain=[0, 1 / 16])
    poly = fit.convert(kind=np.polynomial.Polynomial, domain=[-1, 1], window=[-1, 1])
    return [float(v) for v in poly.coef]


SINE = sine_coefficients()


def scaled_cos(turns, scale):
    r = turns - ((turns + MAGIC) - MAGIC)
    u = jnp.abs(r) - 0.25
    s = u * u
    coefs = [v * scale for v in SINE]
    p = coefs[DEGREE]
    for v in coefs[DEGREE - 1::-1]:
        p = p * s + v
    return p * u


def column(line):
    n = line.shape[1]
    eye = lax.broadcasted_iota(jnp.int32, (128, 128), 0) == lax.broadcasted_iota(jnp.int32, (128, 128), 1)
    parts = []
    for q in range(n // 128):
        square = jnp.broadcast_to(line[:, 128 * q:128 * q + 128], (128, 128))
        parts.append(jnp.sum(jnp.where(eye, square, 0.0), axis=1, keepdims=True))
    return jnp.concatenate(parts, axis=0)


def local_kernel(w_ref, ph_ref, x_ref, *refs, scale):
    o_ref, col_ref = refs[-2:]

    @pl.when(pl.program_id(0) == 0)
    def _():
        col_ref[...] = column(ph_ref[...])

    proj = lax.dot_general(w_ref[...], x_ref[...], NT, preferred_element_type=jnp.float32)
    o_ref[...] = scaled_cos(proj * INV_TURN + col_ref[...], scale).astype(jnp.bfloat16)


def local_features(wt, turns, data, scale, first, blocks, bs, before=None):
    rows, din = wt.shape
    samples = data.shape[0]
    done = [] if before is None else [before]
    return pl.pallas_call(
        functools.partial(local_kernel, scale=scale),
        grid=(blocks,),
        in_specs=[
            pl.BlockSpec((rows, din), lambda i: (0, 0)),
            pl.BlockSpec((1, rows), lambda i: (0, 0)),
            pl.BlockSpec((bs, din), lambda i: (first + i, 0)),
            *[pl.BlockSpec(memory_space=pl.ANY) for _ in done],
        ],
        out_specs=pl.BlockSpec((rows, bs), lambda i: (0, first + i)),
        out_shape=jax.ShapeDtypeStruct((rows, samples), jnp.bfloat16),
        scratch_shapes=[pltpu.VMEM((rows, 1), jnp.float32)],
        input_output_aliases={3: 0} if done else {},
        cost_estimate=pl.CostEstimate(flops=2 * rows * blocks * bs * din, bytes_accessed=3 * blocks * bs * din, transcendentals=0),
        name="local_features",
    )(wt, turns, data, *done)


def place_of(feat):
    return lax.div(feat, 2 * SIDE), lax.rem(lax.div(feat, 2), SIDE), lax.rem(feat, 2)


def gram_kernel(feat_ref, *refs, scale, sub):
    slots, (x_ref, f_ref, e_ref, s_ref, d_ref, v_ref, acc_ref, ph_ref, panel_ref) = refs[:8], refs[8:]
    i = pl.program_id(0)
    rows = s_ref.shape[0]
    y, x, c = place_of(feat_ref[0])
    first = pl.multiple_of(feat_ref[0] * 16, 16)

    def sixteen(p):
        within = pl.ds(pl.multiple_of(lax.rem(first, 256), 16), 16)
        return v_ref[p + lax.div(first, 256), within, :]

    def add(cols, left, right, sign):
        out = lax.dot_general(left, right, NT, preferred_element_type=jnp.float32)
        s_ref[:, cols] += sign * out[:rows]
        acc_ref[:, cols] += sign * out[rows:]

    @pl.when(i == 0)
    def _():
        for k in range(SIDE):
            along_x = lax.rem(x - k + SIDE, SIDE)
            along_y = SIDE + lax.rem(y - k + SIDE, SIDE)
            v_ref[jnp.where(c == 0, along_x, along_y)] = slots[k][...]
            v_ref[jnp.where(c == 0, along_y, along_x)] = slots[SIDE + k][...]
        tail = v_ref[0, 256:256 + EXTRA, :].astype(jnp.float32)
        ph_ref[...] = column((tail[0:1] + tail[1:2]) + tail[2:3])
        s_ref[...] = jnp.zeros_like(s_ref)
        acc_ref[...] = jnp.zeros_like(acc_ref)

    for chunk in range(3):
        @pl.when(i == chunk)
        def _(chunk=chunk):
            left = jnp.concatenate([e_ref[...], sixteen(2 + 2 * chunk)], axis=0)
            for h in range(2):
                add(slice(256 * h, 256 * h + 256), left, v_ref[2 + 2 * chunk + h, :256, :], -1.0)

    for j in range(x_ref.shape[0] // sub):
        at = slice(j * sub, j * sub + sub)
        for h in range(2):
            half = slice(256 * h, 256 * h + 256)
            proj = lax.dot_general(v_ref[h, :256, :], x_ref[at, :], NT, preferred_element_type=jnp.float32)
            panel_ref[j, half, :] = scaled_cos(proj * INV_TURN + ph_ref[half, :], scale).astype(jnp.bfloat16)
        mine = panel_ref[j, pl.ds(first, 16), :]
        left = jnp.concatenate([f_ref[:, at], mine], axis=0)
        for h in range(2):
            half = slice(256 * h, 256 * h + 256)
            add(half, left, panel_ref[j, half, :], 1.0)

    @pl.when(i == pl.num_programs(0) - 1)
    def _():
        for k in range(d_ref.shape[0]):
            d_ref[k] = acc_ref[...]


def gram(feat, slots, data, local, earlier, scale, copies, bs=1024, sub=512):
    rows = earlier.shape[0]
    samples, din = data.shape
    return pl.pallas_call(
        functools.partial(gram_kernel, scale=scale, sub=sub),
        grid=(samples // bs,),
        in_specs=[
            pl.BlockSpec(memory_space=pltpu.SMEM),
            *[pl.BlockSpec(v.shape, lambda i: (0, 0)) for v in slots],
            pl.BlockSpec((bs, din), lambda i: (i, 0)),
            pl.BlockSpec((rows, bs), lambda i: (0, i)),
            pl.BlockSpec((rows, PANEL), lambda i: (0, jnp.minimum(i, 2))),
        ],
        out_specs=[
            pl.BlockSpec((rows, PANEL), lambda i: (0, 0)),
            pl.BlockSpec((copies, 16, PANEL), lambda i: (0, 0, 0)),
        ],
        out_shape=[
            jax.ShapeDtypeStruct((rows, PANEL), jnp.float32),
            jax.ShapeDtypeStruct((copies, 16, PANEL), jnp.float32),
        ],
        scratch_shapes=[
            pltpu.VMEM((2 * SIDE, *slots[0].shape), jnp.bfloat16),
            pltpu.VMEM((16, PANEL), jnp.float32),
            pltpu.VMEM((PANEL, 1), jnp.float32),
            pltpu.VMEM((bs // sub, PANEL, sub), jnp.bfloat16),
        ],
        cost_estimate=pl.CostEstimate(flops=8 << 30, bytes_accessed=16 << 20, transcendentals=0),
        name="gram",
    )(feat, *slots, data, local, earlier)


def split2(v):
    high = v.astype(jnp.bfloat16)
    return high, (v - high.astype(jnp.float32)).astype(jnp.bfloat16)


def split3(v):
    high = v.astype(jnp.bfloat16)
    rest = v - high.astype(jnp.float32)
    mid = rest.astype(jnp.bfloat16)
    return high, mid, (rest - mid.astype(jnp.float32)).astype(jnp.bfloat16)


def spread(block, j):
    return jnp.broadcast_to(block[:, j:j + 1], (8, 128))


def block_inverse(n_ref, lb_ref):
    sub = lax.broadcasted_iota(jnp.int32, (8, 128), 0)
    lane = lax.broadcasted_iota(jnp.int32, (8, 128), 1)

    def step(s, carry):
        rows0, rows1, left, right = carry
        k = pl.multiple_of(s * 8, 8)
        shift = jnp.where(s == 0, 0, 128 - k)
        n_ref[...] -= lax.dot_general(left, right, TN, preferred_element_type=jnp.float32)
        pivot = pltpu.roll(rows0, shift, 1)
        a = [[None] * 8 for _ in range(8)]
        for j in range(8):
            col = spread(pivot, j)
            for i in range(j, 8):
                a[i][j] = jnp.broadcast_to(col[i:i + 1, :], (8, 128))
        low = [[None] * 8 for _ in range(8)]
        root = []
        for j in range(8):
            inverse = 1.0 / a[j][j]
            root.append(lax.rsqrt(a[j][j]))
            for i in range(j + 1, 8):
                low[i][j] = a[i][j] * inverse
            for i in range(j + 1, 8):
                for m in range(j + 1, i + 1):
                    a[i][m] = a[i][m] - low[i][j] * a[m][j]
        t = [[None] * 8 for _ in range(8)]
        for j in range(8):
            t[j][j] = root[j]
            for i in range(j + 1, 8):
                acc = low[i][j]
                for m in range(j + 1, i):
                    acc = acc + low[i][m] * t[m][j]
                t[i][j] = -acc
        for j in range(8):
            for i in range(j + 1, 8):
                t[i][j] = root[i] * t[i][j]
        w0 = jnp.zeros((8, 128), jnp.float32)
        w1 = jnp.zeros((8, 128), jnp.float32)
        for j in range(8):
            col = jnp.where(sub == j, t[j][j], 0.0)
            for i in range(j + 1, 8):
                col = jnp.where(sub == i, t[i][j], col)
            w0 = w0 + col * jnp.broadcast_to(rows0[j:j + 1, :], (8, 128))
            w1 = w1 + col * jnp.broadcast_to(rows1[j:j + 1, :], (8, 128))
        lb_ref[pl.ds(k, 8), :] = w1
        after = jnp.minimum(k + 8, 120)
        after = pl.multiple_of(after, 8)
        next0 = n_ref[pl.ds(after, 8), :128]
        next1 = n_ref[pl.ds(after, 8), 128:]
        cross = pltpu.roll(next0, shift, 1)
        cols = [spread(cross, m) for m in range(8)]
        for j in range(8):
            factor = t[j][0] * cols[0]
            for m in range(1, j + 1):
                factor = factor + t[j][m] * cols[m]
            next0 = next0 - factor * jnp.broadcast_to(w0[j:j + 1, :], (8, 128))
            next1 = next1 - factor * jnp.broadcast_to(w1[j:j + 1, :], (8, 128))
        gh, gm, gl = split3(jnp.where(lane >= k + 8, w0, 0.0))
        wh, wm, wl = split3(jnp.concatenate([w0, w1], axis=1))
        left = jnp.concatenate([gh, gh, gm, gh, gm, gl], axis=0)
        right = jnp.concatenate([wh, wm, wh, wl, wm, wh], axis=0)
        return next0, next1, left, right

    start = (
        n_ref[:8, :128],
        n_ref[:8, 128:],
        jnp.zeros((48, 128), jnp.bfloat16),
        jnp.zeros((48, 256), jnp.bfloat16),
    )
    lax.fori_loop(0, 16, step, start)


def factor_kernel(ridge_ref, d_ref, out_ref, m_ref, j_ref, n_ref, lb_ref):
    n = PANEL
    eye = lax.broadcasted_iota(jnp.int32, (n, n), 0) == lax.broadcasted_iota(jnp.int32, (n, n), 1)
    m_ref[...] = d_ref[...].reshape(n, n) + jnp.where(eye, ridge_ref[0], 0.0)
    j_ref[...] = jnp.where(eye, 1.0, 0.0)
    out_ref[...] = jnp.zeros((n, n), jnp.float32)
    small = lax.broadcasted_iota(jnp.int32, (128, 128), 0) == lax.broadcasted_iota(jnp.int32, (128, 128), 1)
    for b in range(n // 128):
        r0, r1 = 128 * b, 128 * b + 128
        n_ref[:, :128] = m_ref[r0:r1, r0:r1]
        n_ref[:, 128:] = jnp.where(small, 1.0, 0.0)
        block_inverse(n_ref, lb_ref)
        lb = lb_ref[...]
        jb = jnp.dot(lb, j_ref[r0:r1, :r1], precision=HIGHEST, preferred_element_type=jnp.float32)
        out_ref[r0:r1, :r1] = jb
        if r1 < n:
            r = jnp.dot(lb, m_ref[r0:r1, r1:], precision=HIGHEST, preferred_element_type=jnp.float32)
            m_ref[r1:, r1:] -= lax.dot_general(r, r, TN, precision=HIGHEST, preferred_element_type=jnp.float32)
            j_ref[r1:, :r1] -= lax.dot_general(r, jb, TN, precision=HIGHEST, preferred_element_type=jnp.float32)


def factor_inverse(ridge, d):
    n = PANEL
    return pl.pallas_call(
        factor_kernel,
        out_shape=jax.ShapeDtypeStruct((n, n), jnp.float32),
        in_specs=[pl.BlockSpec(memory_space=pltpu.SMEM), pl.BlockSpec(memory_space=pltpu.VMEM)],
        out_specs=pl.BlockSpec(memory_space=pltpu.VMEM),
        scratch_shapes=[
            pltpu.VMEM((n, n), jnp.float32),
            pltpu.VMEM((n, n), jnp.float32),
            pltpu.VMEM((128, 256), jnp.float32),
            pltpu.VMEM((128, 128), jnp.float32),
        ],
        cost_estimate=pl.CostEstimate(flops=8 << 30, bytes_accessed=2 << 20, transcendentals=0),
        name="factor_inverse",
    )(ridge, d)


def solve_kernel(feat_ref, ridge_ref, s_ref, inv_ref, o_ref, *, rows):
    bs = s_ref.shape[0]
    row_ids = feat_ref[0] * rows + pl.program_id(0) * bs + lax.broadcasted_iota(jnp.int32, (bs, PANEL), 0)
    hit = row_ids == lax.broadcasted_iota(jnp.int32, (bs, PANEL), 1)
    sh, sl = split2(s_ref[...] + jnp.where(hit, ridge_ref[0], 0.0))
    for b in range(PANEL // 256):
        r0, r1 = 256 * b, 256 * b + 256
        lh, ll = split2(inv_ref[r0:r1, :r1])
        out = lax.dot_general(sh[:, :r1], ll, NT, preferred_element_type=jnp.float32)
        out += lax.dot_general(sl[:, :r1], lh, NT, preferred_element_type=jnp.float32)
        o_ref[:, r0:r1] = out + lax.dot_general(sh[:, :r1], lh, NT, preferred_element_type=jnp.float32)


def solve(feat, ridge, s, inverse, bs=256):
    rows = s.shape[0]
    smem = pl.BlockSpec(memory_space=pltpu.SMEM)
    return pl.pallas_call(
        functools.partial(solve_kernel, rows=rows),
        grid=(rows // bs,),
        out_shape=jax.ShapeDtypeStruct(s.shape, jnp.float32),
        in_specs=[smem, smem, pl.BlockSpec((bs, PANEL), lambda i: (i, 0)), pl.BlockSpec((PANEL, PANEL), lambda i: (0, 0))],
        out_specs=pl.BlockSpec((bs, PANEL), lambda i: (i, 0)),
        cost_estimate=pl.CostEstimate(flops=6 * rows * PANEL * PANEL, bytes_accessed=4 << 20, transcendentals=0),
        name="solve",
    )(feat, ridge, s, inverse)


def feat_of(y, x, c):
    return ((y % SIDE) * SIDE + x % SIDE) * 2 + c


def permute(value, pairs):
    return lax.ppermute(value, "feat", pairs)


def share_panel(weights, earlier, tail, y, x, c):
    side = range(SIDE)
    root = (feat_of(0, 0, 0), feat_of(0, 0, 1))
    other = permute(earlier[:PANEL, PANEL:3 * PANEL], [root])

    def first_half(k):
        return weights[256 * k:256 * k + 256] if k < 2 else earlier[256 * (k - 2):256 * (k - 1), :PANEL]

    def last_half(k):
        return other[256 * (k % 2):256 * (k % 2) + 256, PANEL * (k // 2):PANEL * (k // 2) + PANEL]

    half = [jnp.where(c == 0, first_half(k), last_half(k)) for k in side]
    got = [permute(half[k], [(root[0], feat_of(0, k, 0)), (root[1], feat_of(k, 0, 1))]) for k in (2, 1, 3)]
    held = jnp.where((x == 0) & (y == 0), half[0], got[0] + got[1] + got[2])
    held = jnp.concatenate([held, tail])
    got = [
        permute(
            held,
            [(feat_of(0, j, 0), feat_of(k, j, 0)) for j in side] + [(feat_of(j, 0, 1), feat_of(j, k, 1)) for j in side],
        )
        for k in (2, 1, 3)
    ]
    held = jnp.where(jnp.where(c == 0, y, x) == 0, held, got[0] + got[1] + got[2])
    own = [held] + [
        permute(
            held,
            [(feat_of(i, j, 0), feat_of(i, j + k, 0)) for i in side for j in side]
            + [(feat_of(i, j, 1), feat_of(i + k, j, 1)) for i in side for j in side],
        )
        for k in (1, 2, 3)
    ]
    partner = [permute(own[k], [(i, i ^ 1) for i in range(2 * SIDE * SIDE)]) for k in side]
    return own + partner


def on_device(data, omega, phase, earlier, ridge):
    samp, planes = lax.axis_size("samp"), lax.axis_size("feat")
    scale = math.sqrt(2.0 / (data.shape[0] * samp))
    feat = lax.axis_index("feat")
    y, x, c = place_of(feat)
    feat = feat.reshape(1)

    weights = omega.T
    turns = phase * INV_TURN
    high = lax.reduce_precision(turns, 8, 7)
    mid = lax.reduce_precision(turns - high, 8, 7)
    low = turns - high - mid
    tail = jnp.stack([high[:PANEL], mid[:PANEL], low[:PANEL]]).astype(jnp.bfloat16)
    tail = jnp.concatenate([tail, jnp.zeros((EXTRA - 3, PANEL), jnp.bfloat16)])
    slots = share_panel(weights, earlier, tail, y, x, c)

    local = None
    blocks = data.shape[0] // SAMPLE_BLOCK
    for part, first in enumerate((0, blocks // 4, blocks // 2)):
        count = blocks // 2 if part == 2 else blocks // 4
        local = local_features(weights, turns[None], data, scale, first, count, SAMPLE_BLOCK, local)
    s, d = gram(feat, slots, data, local, earlier, scale, samp)
    summed = lax.psum(s, "samp")
    d = lax.all_to_all(d, "samp", 0, 0).sum(0)
    d = lax.all_to_all(jnp.broadcast_to(d, (planes, 16, PANEL)), "feat", 0, 0)
    inverse = factor_inverse(ridge, d)
    return solve(feat, ridge, summed, inverse)


def solution(mesh):
    in_specs = (P("samp", None), P(None, "feat"), P("feat"), P("feat", "samp"), P())
    out_specs = P("feat", None)
    return jax.shard_map(on_device, mesh=mesh, in_specs=in_specs, out_specs=out_specs, check_vma=False)
```

```python
import functools
import math

import jax
import jax.numpy as jnp
import numpy as np
from jax import lax
from jax.experimental import pallas as pl
from jax.experimental.pallas import tpu as pltpu
from jax.sharding import PartitionSpec as P


PANEL = 512
SIDE = 4
SAMPLE_BLOCK = 512
EXTRA = 16
HIGHEST = lax.Precision.HIGHEST
NT = (((1,), (1,)), ((), ()))
TN = (((0,), (0,)), ((), ()))
INV_TURN = 1.0 / (2.0 * math.pi)
DEGREE = 3


def sine_coefficients():
    u = np.cos(np.pi * (np.arange(4000) + 0.5) / 4000) * 0.25
    fit = np.polynomial.chebyshev.Chebyshev.fit(u * u, -np.sin(2 * np.pi * u) / u, DEGREE, domain=[0, 1 / 16])
    poly = fit.convert(kind=np.polynomial.Polynomial, domain=[-1, 1], window=[-1, 1])
    return [float(v) for v in poly.coef]


SINE = sine_coefficients()


def scaled_cos(turns, scale):
    r = turns - jnp.round(turns)
    u = jnp.abs(r) - 0.25
    s = u * u
    coefs = [v * scale for v in SINE]
    p = coefs[DEGREE]
    for v in coefs[DEGREE - 1::-1]:
        p = p * s + v
    return p * u


def column(line):
    n = line.shape[1]
    eye = lax.broadcasted_iota(jnp.int32, (128, 128), 0) == lax.broadcasted_iota(jnp.int32, (128, 128), 1)
    parts = []
    for q in range(n // 128):
        square = jnp.broadcast_to(line[:, 128 * q:128 * q + 128], (128, 128))
        parts.append(jnp.sum(jnp.where(eye, square, 0.0), axis=1, keepdims=True))
    return jnp.concatenate(parts, axis=0)


def local_kernel(w_ref, ph_ref, x_ref, *refs, scale):
    o_ref, col_ref = refs[-2:]

    @pl.when(pl.program_id(0) == 0)
    def _():
        col_ref[...] = column(ph_ref[...])

    for r in range(w_ref.shape[0] // 256):
        part = slice(256 * r, 256 * r + 256)
        proj = lax.dot_general(w_ref[part, :], x_ref[...], NT, preferred_element_type=jnp.float32)
        o_ref[part, :] = scaled_cos(proj * INV_TURN + col_ref[part, :], scale).astype(jnp.bfloat16)


def local_features(wt, turns, data, scale, first, blocks, bs, before=None):
    rows, din = wt.shape
    samples = data.shape[0]
    done = [] if before is None else [before]
    return pl.pallas_call(
        functools.partial(local_kernel, scale=scale),
        grid=(blocks,),
        in_specs=[
            pl.BlockSpec((rows, din), lambda i: (0, 0)),
            pl.BlockSpec((1, rows), lambda i: (0, 0)),
            pl.BlockSpec((bs, din), lambda i: (first + i, 0)),
            *[pl.BlockSpec(memory_space=pl.ANY) for _ in done],
        ],
        out_specs=pl.BlockSpec((rows, bs), lambda i: (0, first + i)),
        out_shape=jax.ShapeDtypeStruct((rows, samples), jnp.bfloat16),
        scratch_shapes=[pltpu.VMEM((rows, 1), jnp.float32)],
        input_output_aliases={3: 0} if done else {},
        cost_estimate=pl.CostEstimate(flops=2 * rows * blocks * bs * din, bytes_accessed=3 * blocks * bs * din, transcendentals=0),
        name="local_features",
    )(wt, turns, data, *done)


def place_of(feat):
    return lax.div(feat, 2 * SIDE), lax.rem(lax.div(feat, 2), SIDE), lax.rem(feat, 2)


def gram_kernel(feat_ref, *refs, scale, sub):
    slots, (x_ref, f_ref, e_ref, s_ref, d_ref, v_ref, acc_ref, ph_ref, panel_ref) = refs[:8], refs[8:]
    i = pl.program_id(0)
    rows = s_ref.shape[0]
    y, x, c = place_of(feat_ref[0])
    first = pl.multiple_of(feat_ref[0] * 16, 16)

    def sixteen(p):
        within = pl.ds(pl.multiple_of(lax.rem(first, 256), 16), 16)
        return v_ref[p + lax.div(first, 256), within, :]

    def add(cols, left, right, sign):
        out = lax.dot_general(left, right, NT, preferred_element_type=jnp.float32)
        s_ref[:, cols] += sign * out[:rows]
        acc_ref[:, cols] += sign * out[rows:]

    @pl.when(i == 0)
    def _():
        for k in range(SIDE):
            along_x = lax.rem(x - k + SIDE, SIDE)
            along_y = SIDE + lax.rem(y - k + SIDE, SIDE)
            v_ref[jnp.where(c == 0, along_x, along_y)] = slots[k][...]
            v_ref[jnp.where(c == 0, along_y, along_x)] = slots[SIDE + k][...]
        tail = v_ref[0, 256:256 + EXTRA, :].astype(jnp.float32)
        ph_ref[...] = column((tail[0:1] + tail[1:2]) + tail[2:3])
        s_ref[...] = jnp.zeros_like(s_ref)
        acc_ref[...] = jnp.zeros_like(acc_ref)

    for chunk in range(3):
        @pl.when(i == chunk)
        def _(chunk=chunk):
            left = jnp.concatenate([e_ref[...], sixteen(2 + 2 * chunk)], axis=0)
            for h in range(2):
                add(slice(256 * h, 256 * h + 256), left, v_ref[2 + 2 * chunk + h, :256, :], -1.0)

    for j in range(x_ref.shape[0] // sub):
        at = slice(j * sub, j * sub + sub)
        for h in range(2):
            half = slice(256 * h, 256 * h + 256)
            proj = lax.dot_general(v_ref[h, :256, :], x_ref[at, :], NT, preferred_element_type=jnp.float32)
            panel_ref[j, half, :] = scaled_cos(proj * INV_TURN + ph_ref[half, :], scale).astype(jnp.bfloat16)
        mine = panel_ref[j, pl.ds(first, 16), :]
        left = jnp.concatenate([f_ref[:, at], mine], axis=0)
        for h in range(2):
            half = slice(256 * h, 256 * h + 256)
            add(half, left, panel_ref[j, half, :], 1.0)

    @pl.when(i == pl.num_programs(0) - 1)
    def _():
        for k in range(d_ref.shape[0]):
            d_ref[k] = acc_ref[...]


def gram(feat, slots, data, local, earlier, scale, copies, bs=1024, sub=512):
    rows = earlier.shape[0]
    samples, din = data.shape
    return pl.pallas_call(
        functools.partial(gram_kernel, scale=scale, sub=sub),
        grid=(samples // bs,),
        in_specs=[
            pl.BlockSpec(memory_space=pltpu.SMEM),
            *[pl.BlockSpec(memory_space=pltpu.VMEM) for _ in slots],
            pl.BlockSpec((bs, din), lambda i: (i, 0)),
            pl.BlockSpec((rows, bs), lambda i: (0, i)),
            pl.BlockSpec((rows, PANEL), lambda i: (0, jnp.minimum(i, 2))),
        ],
        out_specs=[
            pl.BlockSpec((rows, PANEL), lambda i: (0, 0)),
            pl.BlockSpec((copies, 16, PANEL), lambda i: (0, 0, 0)),
        ],
        out_shape=[
            jax.ShapeDtypeStruct((rows, PANEL), jnp.float32),
            jax.ShapeDtypeStruct((copies, 16, PANEL), jnp.float32),
        ],
        scratch_shapes=[
            pltpu.VMEM((2 * SIDE, *slots[0].shape), jnp.bfloat16),
            pltpu.VMEM((16, PANEL), jnp.float32),
            pltpu.VMEM((PANEL, 1), jnp.float32),
            pltpu.VMEM((bs // sub, PANEL, sub), jnp.bfloat16),
        ],
        cost_estimate=pl.CostEstimate(flops=8 << 30, bytes_accessed=16 << 20, transcendentals=0),
        compiler_params=pltpu.CompilerParams(vmem_limit_bytes=50 << 20),
        name="gram",
    )(feat, *slots, data, local, earlier)


def split2(v):
    high = v.astype(jnp.bfloat16)
    return high, (v - high.astype(jnp.float32)).astype(jnp.bfloat16)


def split3(v):
    high = v.astype(jnp.bfloat16)
    rest = v - high.astype(jnp.float32)
    mid = rest.astype(jnp.bfloat16)
    return high, mid, (rest - mid.astype(jnp.float32)).astype(jnp.bfloat16)


def spread(block, j):
    return jnp.broadcast_to(block[:, j:j + 1], (8, 128))


def block_inverse(n_ref, lb_ref):
    sub = lax.broadcasted_iota(jnp.int32, (8, 128), 0)
    lane = lax.broadcasted_iota(jnp.int32, (8, 128), 1)

    def step(s, carry):
        rows0, rows1, left, right = carry
        k = pl.multiple_of(s * 8, 8)
        shift = jnp.where(s == 0, 0, 128 - k)
        n_ref[...] -= lax.dot_general(left, right, TN, preferred_element_type=jnp.float32)
        pivot = pltpu.roll(rows0, shift, 1)
        a = [[None] * 8 for _ in range(8)]
        for j in range(8):
            col = spread(pivot, j)
            for i in range(j, 8):
                a[i][j] = jnp.broadcast_to(col[i:i + 1, :], (8, 128))
        low = [[None] * 8 for _ in range(8)]
        root = []
        for j in range(8):
            inverse = 1.0 / a[j][j]
            root.append(lax.rsqrt(a[j][j]))
            for i in range(j + 1, 8):
                low[i][j] = a[i][j] * inverse
            for i in range(j + 1, 8):
                for m in range(j + 1, i + 1):
                    a[i][m] = a[i][m] - low[i][j] * a[m][j]
        t = [[None] * 8 for _ in range(8)]
        for j in range(8):
            t[j][j] = root[j]
            for i in range(j + 1, 8):
                acc = low[i][j]
                for m in range(j + 1, i):
                    acc = acc + low[i][m] * t[m][j]
                t[i][j] = -acc
        for j in range(8):
            for i in range(j + 1, 8):
                t[i][j] = root[i] * t[i][j]
        w0 = jnp.zeros((8, 128), jnp.float32)
        w1 = jnp.zeros((8, 128), jnp.float32)
        for j in range(8):
            col = jnp.where(sub == j, t[j][j], 0.0)
            for i in range(j + 1, 8):
                col = jnp.where(sub == i, t[i][j], col)
            w0 = w0 + col * jnp.broadcast_to(rows0[j:j + 1, :], (8, 128))
            w1 = w1 + col * jnp.broadcast_to(rows1[j:j + 1, :], (8, 128))
        lb_ref[pl.ds(k, 8), :] = w1
        after = jnp.minimum(k + 8, 120)
        after = pl.multiple_of(after, 8)
        next0 = n_ref[pl.ds(after, 8), :128]
        next1 = n_ref[pl.ds(after, 8), 128:]
        cross = pltpu.roll(next0, shift, 1)
        cols = [spread(cross, m) for m in range(8)]
        for j in range(8):
            factor = t[j][0] * cols[0]
            for m in range(1, j + 1):
                factor = factor + t[j][m] * cols[m]
            next0 = next0 - factor * jnp.broadcast_to(w0[j:j + 1, :], (8, 128))
            next1 = next1 - factor * jnp.broadcast_to(w1[j:j + 1, :], (8, 128))
        gh, gm, gl = split3(jnp.where(lane >= k + 8, w0, 0.0))
        wh, wm, wl = split3(jnp.concatenate([w0, w1], axis=1))
        left = jnp.concatenate([gh, gh, gm, gh, gm, gl], axis=0)
        right = jnp.concatenate([wh, wm, wh, wl, wm, wh], axis=0)
        return next0, next1, left, right

    start = (
        n_ref[:8, :128],
        n_ref[:8, 128:],
        jnp.zeros((48, 128), jnp.bfloat16),
        jnp.zeros((48, 256), jnp.bfloat16),
    )
    lax.fori_loop(0, 16, step, start)


def factor_kernel(ridge_ref, d_ref, high_ref, low_ref, m_ref, j_ref, n_ref, lb_ref):
    n = PANEL
    eye = lax.broadcasted_iota(jnp.int32, (n, n), 0) == lax.broadcasted_iota(jnp.int32, (n, n), 1)
    m_ref[...] = d_ref[...].reshape(n, n) + jnp.where(eye, ridge_ref[0], 0.0)
    j_ref[...] = jnp.where(eye, 1.0, 0.0)
    high_ref[...] = jnp.zeros((n, n), jnp.bfloat16)
    low_ref[...] = jnp.zeros((n, n), jnp.bfloat16)
    small = lax.broadcasted_iota(jnp.int32, (128, 128), 0) == lax.broadcasted_iota(jnp.int32, (128, 128), 1)
    for b in range(n // 128):
        r0, r1 = 128 * b, 128 * b + 128
        n_ref[:, :128] = m_ref[r0:r1, r0:r1]
        n_ref[:, 128:] = jnp.where(small, 1.0, 0.0)
        block_inverse(n_ref, lb_ref)
        lb = lb_ref[...]
        jb = jnp.dot(lb, j_ref[r0:r1, :r1], precision=HIGHEST, preferred_element_type=jnp.float32)
        high_ref[r0:r1, :r1], low_ref[r0:r1, :r1] = split2(jb)
        if r1 < n:
            r = jnp.dot(lb, m_ref[r0:r1, r1:], precision=HIGHEST, preferred_element_type=jnp.float32)
            m_ref[r1:, r1:] -= lax.dot_general(r, r, TN, precision=HIGHEST, preferred_element_type=jnp.float32)
            j_ref[r1:, :r1] -= lax.dot_general(r, jb, TN, precision=HIGHEST, preferred_element_type=jnp.float32)


def factor_inverse(ridge, d):
    n = PANEL
    return pl.pallas_call(
        factor_kernel,
        out_shape=[jax.ShapeDtypeStruct((n, n), jnp.bfloat16)] * 2,
        in_specs=[pl.BlockSpec(memory_space=pltpu.SMEM), pl.BlockSpec(memory_space=pltpu.VMEM)],
        out_specs=[pl.BlockSpec(memory_space=pltpu.VMEM)] * 2,
        scratch_shapes=[
            pltpu.VMEM((n, n), jnp.float32),
            pltpu.VMEM((n, n), jnp.float32),
            pltpu.VMEM((128, 256), jnp.float32),
            pltpu.VMEM((128, 128), jnp.float32),
        ],
        cost_estimate=pl.CostEstimate(flops=8 << 30, bytes_accessed=2 << 20, transcendentals=0),
        compiler_params=pltpu.CompilerParams(vmem_limit_bytes=12 << 20),
        name="factor_inverse",
    )(ridge, d)


def solve_kernel(feat_ref, ridge_ref, s_ref, high_ref, low_ref, o_ref, *, rows):
    bs = s_ref.shape[0]
    row_ids = feat_ref[0] * rows + pl.program_id(0) * bs + lax.broadcasted_iota(jnp.int32, (bs, PANEL), 0)
    hit = row_ids == lax.broadcasted_iota(jnp.int32, (bs, PANEL), 1)
    sh, sl = split2(s_ref[...] + jnp.where(hit, ridge_ref[0], 0.0))
    for b in range(PANEL // 256):
        r0, r1 = 256 * b, 256 * b + 256
        out = lax.dot_general(sh[:, :r1], low_ref[r0:r1, :r1], NT, preferred_element_type=jnp.float32)
        out += lax.dot_general(sl[:, :r1], high_ref[r0:r1, :r1], NT, preferred_element_type=jnp.float32)
        o_ref[:, r0:r1] = out + lax.dot_general(sh[:, :r1], high_ref[r0:r1, :r1], NT, preferred_element_type=jnp.float32)


def solve(feat, ridge, s, high, low, bs=384):
    rows = s.shape[0]
    smem = pl.BlockSpec(memory_space=pltpu.SMEM)
    return pl.pallas_call(
        functools.partial(solve_kernel, rows=rows),
        grid=(rows // bs,),
        out_shape=jax.ShapeDtypeStruct(s.shape, jnp.float32),
        in_specs=[smem, smem, pl.BlockSpec((bs, PANEL), lambda i: (i, 0)), *[pl.BlockSpec(memory_space=pltpu.VMEM)] * 2],
        out_specs=pl.BlockSpec((bs, PANEL), lambda i: (i, 0)),
        cost_estimate=pl.CostEstimate(flops=6 * rows * PANEL * PANEL, bytes_accessed=4 << 20, transcendentals=0),
        compiler_params=pltpu.CompilerParams(vmem_limit_bytes=65_600_000),
        name="solve",
    )(feat, ridge, s, high, low)


def feat_of(y, x, c):
    return ((y % SIDE) * SIDE + x % SIDE) * 2 + c


def permute(value, pairs):
    return lax.ppermute(value, "feat", pairs)


def share_panel(weights, earlier, tail, y, x, c):
    side = range(SIDE)
    root = (feat_of(0, 0, 0), feat_of(0, 0, 1))
    other = permute(earlier[:PANEL, PANEL:3 * PANEL], [root])

    def first_half(k):
        return weights[256 * k:256 * k + 256] if k < 2 else earlier[256 * (k - 2):256 * (k - 1), :PANEL]

    def last_half(k):
        return other[256 * (k % 2):256 * (k % 2) + 256, PANEL * (k // 2):PANEL * (k // 2) + PANEL]

    half = [jnp.where(c == 0, first_half(k), last_half(k)) for k in side]
    got = [permute(half[k], [(root[0], feat_of(0, k, 0)), (root[1], feat_of(k, 0, 1))]) for k in (2, 1, 3)]
    held = jnp.where((x == 0) & (y == 0), half[0], got[0] + got[1] + got[2])
    held = jnp.concatenate([held, tail])
    got = [
        permute(
            held,
            [(feat_of(0, j, 0), feat_of(k, j, 0)) for j in side] + [(feat_of(j, 0, 1), feat_of(j, k, 1)) for j in side],
        )
        for k in (2, 1, 3)
    ]
    held = jnp.where(jnp.where(c == 0, y, x) == 0, held, got[0] + got[1] + got[2])
    got = {
        k: permute(
            held,
            [(feat_of(i, j, 0), feat_of(i, j + k, 0)) for i in side for j in side]
            + [(feat_of(i, j, 1), feat_of(i + k, j, 1)) for i in side for j in side],
        )
        for k in (2, 1, 3)
    }
    own = [held, got[1], got[2], got[3]]
    partner = [permute(own[k], [(i, i ^ 1) for i in range(2 * SIDE * SIDE)]) for k in side]
    return own + partner


def on_device(data, omega, phase, earlier, ridge):
    samp, planes = lax.axis_size("samp"), lax.axis_size("feat")
    scale = math.sqrt(2.0 / (data.shape[0] * samp))
    feat = lax.axis_index("feat")
    y, x, c = place_of(feat)
    feat = feat.reshape(1)

    weights = omega.T
    turns = phase * INV_TURN
    first = lax.reduce_precision(turns, 8, 7)
    second = lax.reduce_precision(turns - first, 8, 7)
    third = turns - first - second
    tail = jnp.stack([first[:PANEL], second[:PANEL], third[:PANEL]]).astype(jnp.bfloat16)
    tail = jnp.concatenate([tail, jnp.zeros((EXTRA - 3, PANEL), jnp.bfloat16)])
    slots = share_panel(weights, earlier, tail, y, x, c)

    local = None
    blocks = data.shape[0] // SAMPLE_BLOCK
    edges = (0, blocks // 4, 5 * blocks // 8, blocks)
    for part in range(3):
        count = edges[part + 1] - edges[part]
        local = local_features(weights, turns[None], data, scale, edges[part], count, SAMPLE_BLOCK, local)
    s, d = gram(feat, slots, *[pltpu.with_memory_space_constraint(v, pltpu.HBM) for v in (data, local, earlier)], scale, samp)
    summed = lax.psum(s, "samp")
    d = lax.all_to_all(d, "samp", 0, 0).sum(0)
    d = lax.all_to_all(jnp.broadcast_to(d, (planes, 16, PANEL)), "feat", 0, 0)
    high, low = factor_inverse(ridge, d)
    return solve(feat, ridge, summed, high, low)


def solution(mesh):
    in_specs = (P("samp", None), P(None, "feat"), P("feat"), P("feat", "samp"), P())
    out_specs = P("feat", None)
    return jax.shard_map(on_device, mesh=mesh, in_specs=in_specs, out_specs=out_specs, check_vma=False)
```

```python
import functools
import math

import jax
import jax.numpy as jnp
import numpy as np
from jax import lax
from jax.experimental import pallas as pl
from jax.experimental.pallas import tpu as pltpu
from jax.sharding import PartitionSpec as P


PANEL = 512
SIDE = 4
SAMPLE_BLOCK = 512
EXTRA = 16
HIGHEST = lax.Precision.HIGHEST
NT = (((1,), (1,)), ((), ()))
TN = (((0,), (0,)), ((), ()))
INV_TURN = 1.0 / (2.0 * math.pi)
DEGREE = 3


def sine_coefficients():
    u = np.cos(np.pi * (np.arange(4000) + 0.5) / 4000) * 0.25
    fit = np.polynomial.chebyshev.Chebyshev.fit(u * u, -np.sin(2 * np.pi * u) / u, DEGREE, domain=[0, 1 / 16])
    poly = fit.convert(kind=np.polynomial.Polynomial, domain=[-1, 1], window=[-1, 1])
    return [float(v) for v in poly.coef]


SINE = sine_coefficients()


def scaled_cos(turns, scale):
    r = turns - jnp.round(turns)
    u = jnp.abs(r) - 0.25
    s = u * u
    coefs = [v * scale for v in SINE]
    p = coefs[DEGREE]
    for v in coefs[DEGREE - 1::-1]:
        p = p * s + v
    return p * u


def column(line):
    n = line.shape[1]
    eye = lax.broadcasted_iota(jnp.int32, (128, 128), 0) == lax.broadcasted_iota(jnp.int32, (128, 128), 1)
    parts = []
    for q in range(n // 128):
        square = jnp.broadcast_to(line[:, 128 * q:128 * q + 128], (128, 128))
        parts.append(jnp.sum(jnp.where(eye, square, 0.0), axis=1, keepdims=True))
    return jnp.concatenate(parts, axis=0)


def local_kernel(w_ref, ph_ref, x_ref, *refs, scale):
    o_ref, col_ref = refs[-2:]

    @pl.when(pl.program_id(0) == 0)
    def _():
        col_ref[...] = column(ph_ref[...])

    for r in range(w_ref.shape[0] // 256):
        part = slice(256 * r, 256 * r + 256)
        proj = lax.dot_general(w_ref[part, :], x_ref[...], NT, preferred_element_type=jnp.float32)
        o_ref[part, :] = scaled_cos(proj * INV_TURN + col_ref[part, :], scale).astype(jnp.bfloat16)


def local_features(wt, turns, data, scale, first, blocks, bs, before=None):
    rows, din = wt.shape
    samples = data.shape[0]
    done = [] if before is None else [before]
    return pl.pallas_call(
        functools.partial(local_kernel, scale=scale),
        grid=(blocks,),
        in_specs=[
            pl.BlockSpec((rows, din), lambda i: (0, 0)),
            pl.BlockSpec((1, rows), lambda i: (0, 0)),
            pl.BlockSpec((bs, din), lambda i: (first + i, 0)),
            *[pl.BlockSpec(memory_space=pl.ANY) for _ in done],
        ],
        out_specs=pl.BlockSpec((rows, bs), lambda i: (0, first + i)),
        out_shape=jax.ShapeDtypeStruct((rows, samples), jnp.bfloat16),
        scratch_shapes=[pltpu.VMEM((rows, 1), jnp.float32)],
        input_output_aliases={3: 0} if done else {},
        cost_estimate=pl.CostEstimate(flops=2 * rows * blocks * bs * din, bytes_accessed=3 * blocks * bs * din, transcendentals=0),
        name="local_features",
    )(wt, turns, data, *done)


def place_of(feat):
    return lax.div(feat, 2 * SIDE), lax.rem(lax.div(feat, 2), SIDE), lax.rem(feat, 2)


def gram_kernel(feat_ref, *refs, scale, sub):
    slots, (x_ref, f_ref, e_ref, s_ref, d_ref, v_ref, acc_ref, ph_ref, panel_ref) = refs[:8], refs[8:]
    i = pl.program_id(0)
    rows = s_ref.shape[0]
    y, x, c = place_of(feat_ref[0])
    first = pl.multiple_of(feat_ref[0] * 16, 16)

    def sixteen(p):
        within = pl.ds(pl.multiple_of(lax.rem(first, 256), 16), 16)
        return v_ref[p + lax.div(first, 256), within, :]

    def add(cols, left, right, negate=False):
        out = lax.dot_general(left, right, NT, preferred_element_type=jnp.float32)
        if negate:
            s_ref[:, cols] -= out[:rows]
            acc_ref[:, cols] -= out[rows:]
        else:
            s_ref[:, cols] += out[:rows]
            acc_ref[:, cols] += out[rows:]

    @pl.when(i == 0)
    def _():
        for k in range(SIDE):
            along_x = lax.rem(x - k + SIDE, SIDE)
            along_y = SIDE + lax.rem(y - k + SIDE, SIDE)
            v_ref[jnp.where(c == 0, along_x, along_y)] = slots[k][...]
            v_ref[jnp.where(c == 0, along_y, along_x)] = slots[SIDE + k][...]
        tail = v_ref[0, 256:256 + EXTRA, :].astype(jnp.float32)
        ph_ref[...] = column((tail[0:1] + tail[1:2]) + tail[2:3])
        s_ref[...] = jnp.zeros_like(s_ref)
        acc_ref[...] = jnp.zeros_like(acc_ref)

    for chunk in range(3):
        @pl.when(i == chunk)
        def _(chunk=chunk):
            left = jnp.concatenate([e_ref[...], sixteen(2 + 2 * chunk)], axis=0)
            for h in range(2):
                add(slice(256 * h, 256 * h + 256), left, v_ref[2 + 2 * chunk + h, :256, :], negate=True)

    for j in range(x_ref.shape[0] // sub):
        at = slice(j * sub, j * sub + sub)
        for h in range(2):
            half = slice(256 * h, 256 * h + 256)
            proj = lax.dot_general(v_ref[h, :256, :], x_ref[at, :], NT, preferred_element_type=jnp.float32)
            panel_ref[j, half, :] = scaled_cos(proj * INV_TURN + ph_ref[half, :], scale).astype(jnp.bfloat16)
    for j in range(x_ref.shape[0] // sub):
        at = slice(j * sub, j * sub + sub)
        mine = panel_ref[j, pl.ds(first, 16), :]
        left = jnp.concatenate([f_ref[:, at], mine], axis=0)
        for h in range(2):
            half = slice(256 * h, 256 * h + 256)
            add(half, left, panel_ref[j, half, :])

    @pl.when(i == pl.num_programs(0) - 1)
    def _():
        for k in range(d_ref.shape[0]):
            d_ref[k] = acc_ref[...]


def gram(feat, slots, data, local, earlier, scale, copies, bs=1024, sub=512):
    rows = earlier.shape[0]
    samples, din = data.shape
    return pl.pallas_call(
        functools.partial(gram_kernel, scale=scale, sub=sub),
        grid=(samples // bs,),
        in_specs=[
            pl.BlockSpec(memory_space=pltpu.SMEM),
            *[pl.BlockSpec(memory_space=pltpu.VMEM) for _ in slots],
            pl.BlockSpec((bs, din), lambda i: (i, 0)),
            pl.BlockSpec((rows, bs), lambda i: (0, i)),
            pl.BlockSpec((rows, PANEL), lambda i: (0, jnp.minimum(i, 2))),
        ],
        out_specs=[
            pl.BlockSpec((rows, PANEL), lambda i: (0, 0)),
            pl.BlockSpec((copies, 16, PANEL), lambda i: (0, 0, 0)),
        ],
        out_shape=[
            jax.ShapeDtypeStruct((rows, PANEL), jnp.float32),
            jax.ShapeDtypeStruct((copies, 16, PANEL), jnp.float32),
        ],
        scratch_shapes=[
            pltpu.VMEM((2 * SIDE, *slots[0].shape), jnp.bfloat16),
            pltpu.VMEM((16, PANEL), jnp.float32),
            pltpu.VMEM((PANEL, 1), jnp.float32),
            pltpu.VMEM((bs // sub, PANEL, sub), jnp.bfloat16),
        ],
        cost_estimate=pl.CostEstimate(flops=8 << 30, bytes_accessed=16 << 20, transcendentals=0),
        compiler_params=pltpu.CompilerParams(vmem_limit_bytes=50 << 20),
        name="gram",
    )(feat, *slots, data, local, earlier)


def split2(v):
    high = v.astype(jnp.bfloat16)
    return high, (v - high.astype(jnp.float32)).astype(jnp.bfloat16)


def split3(v):
    high = v.astype(jnp.bfloat16)
    rest = v - high.astype(jnp.float32)
    mid = rest.astype(jnp.bfloat16)
    return high, mid, (rest - mid.astype(jnp.float32)).astype(jnp.bfloat16)


def spread(block, j):
    return jnp.broadcast_to(block[:, j:j + 1], (8, 128))


def block_inverse(n_ref, lb_ref):
    sub = lax.broadcasted_iota(jnp.int32, (8, 128), 0)
    lane = lax.broadcasted_iota(jnp.int32, (8, 128), 1)

    def step(s, carry):
        rows0, rows1, left, right = carry
        k = pl.multiple_of(s * 8, 8)
        shift = jnp.where(s == 0, 0, 128 - k)
        n_ref[...] -= lax.dot_general(left, right, TN, preferred_element_type=jnp.float32)
        pivot = pltpu.roll(rows0, shift, 1)
        a = [[None] * 8 for _ in range(8)]
        for j in range(8):
            col = spread(pivot, j)
            for i in range(j, 8):
                a[i][j] = jnp.broadcast_to(col[i:i + 1, :], (8, 128))
        low = [[None] * 8 for _ in range(8)]
        root = []
        for j in range(8):
            inverse = 1.0 / a[j][j]
            root.append(lax.rsqrt(a[j][j]))
            for i in range(j + 1, 8):
                low[i][j] = a[i][j] * inverse
            for i in range(j + 1, 8):
                for m in range(j + 1, i + 1):
                    a[i][m] = a[i][m] - low[i][j] * a[m][j]
        t = [[None] * 8 for _ in range(8)]
        for j in range(8):
            t[j][j] = root[j]
            for i in range(j + 1, 8):
                acc = low[i][j]
                for m in range(j + 1, i):
                    acc = acc + low[i][m] * t[m][j]
                t[i][j] = -acc
        for j in range(8):
            for i in range(j + 1, 8):
                t[i][j] = root[i] * t[i][j]
        w0 = jnp.zeros((8, 128), jnp.float32)
        w1 = jnp.zeros((8, 128), jnp.float32)
        for j in range(8):
            col = jnp.where(sub == j, t[j][j], 0.0)
            for i in range(j + 1, 8):
                col = jnp.where(sub == i, t[i][j], col)
            w0 = w0 + col * jnp.broadcast_to(rows0[j:j + 1, :], (8, 128))
            w1 = w1 + col * jnp.broadcast_to(rows1[j:j + 1, :], (8, 128))
        lb_ref[pl.ds(k, 8), :] = w1
        after = jnp.minimum(k + 8, 120)
        after = pl.multiple_of(after, 8)
        next0 = n_ref[pl.ds(after, 8), :128]
        next1 = n_ref[pl.ds(after, 8), 128:]
        cross = pltpu.roll(next0, shift, 1)
        cols = [spread(cross, m) for m in range(8)]
        for j in range(8):
            factor = t[j][0] * cols[0]
            for m in range(1, j + 1):
                factor = factor + t[j][m] * cols[m]
            next0 = next0 - factor * jnp.broadcast_to(w0[j:j + 1, :], (8, 128))
            next1 = next1 - factor * jnp.broadcast_to(w1[j:j + 1, :], (8, 128))
        gh, gm, gl = split3(jnp.where(lane >= k + 8, w0, 0.0))
        wh, wm, wl = split3(jnp.concatenate([w0, w1], axis=1))
        left = jnp.concatenate([gh, gh, gm, gh, gm, gl], axis=0)
        right = jnp.concatenate([wh, wm, wh, wl, wm, wh], axis=0)
        return next0, next1, left, right

    start = (
        n_ref[:8, :128],
        n_ref[:8, 128:],
        jnp.zeros((48, 128), jnp.bfloat16),
        jnp.zeros((48, 256), jnp.bfloat16),
    )
    lax.fori_loop(0, 16, step, start)


def factor_kernel(ridge_ref, d_ref, high_ref, low_ref, m_ref, j_ref, n_ref, lb_ref):
    n = PANEL
    eye = lax.broadcasted_iota(jnp.int32, (n, n), 0) == lax.broadcasted_iota(jnp.int32, (n, n), 1)
    m_ref[...] = d_ref[...].reshape(n, n) + jnp.where(eye, ridge_ref[0], 0.0)
    j_ref[...] = jnp.where(eye, 1.0, 0.0)
    high_ref[...] = jnp.zeros((n, n), jnp.bfloat16)
    low_ref[...] = jnp.zeros((n, n), jnp.bfloat16)
    small = lax.broadcasted_iota(jnp.int32, (128, 128), 0) == lax.broadcasted_iota(jnp.int32, (128, 128), 1)
    for b in range(n // 128):
        r0, r1 = 128 * b, 128 * b + 128
        n_ref[:, :128] = m_ref[r0:r1, r0:r1]
        n_ref[:, 128:] = jnp.where(small, 1.0, 0.0)
        block_inverse(n_ref, lb_ref)
        lb = lb_ref[...]
        jb = jnp.dot(lb, j_ref[r0:r1, :r1], precision=HIGHEST, preferred_element_type=jnp.float32)
        high_ref[r0:r1, :r1], low_ref[r0:r1, :r1] = split2(jb)
        if r1 < n:
            r = jnp.dot(lb, m_ref[r0:r1, r1:], precision=HIGHEST, preferred_element_type=jnp.float32)
            m_ref[r1:, r1:] -= lax.dot_general(r, r, TN, precision=HIGHEST, preferred_element_type=jnp.float32)
            j_ref[r1:, :r1] -= lax.dot_general(r, jb, TN, precision=HIGHEST, preferred_element_type=jnp.float32)


def factor_inverse(ridge, d):
    n = PANEL
    return pl.pallas_call(
        factor_kernel,
        out_shape=[jax.ShapeDtypeStruct((n, n), jnp.bfloat16)] * 2,
        in_specs=[pl.BlockSpec(memory_space=pltpu.SMEM), pl.BlockSpec(memory_space=pltpu.VMEM)],
        out_specs=[pl.BlockSpec(memory_space=pltpu.VMEM)] * 2,
        scratch_shapes=[
            pltpu.VMEM((n, n), jnp.float32),
            pltpu.VMEM((n, n), jnp.float32),
            pltpu.VMEM((128, 256), jnp.float32),
            pltpu.VMEM((128, 128), jnp.float32),
        ],
        cost_estimate=pl.CostEstimate(flops=8 << 30, bytes_accessed=2 << 20, transcendentals=0),
        compiler_params=pltpu.CompilerParams(vmem_limit_bytes=12 << 20),
        name="factor_inverse",
    )(ridge, d)


def solve_kernel(feat_ref, ridge_ref, s_ref, high_ref, low_ref, o_ref, *, rows):
    bs = s_ref.shape[0]
    row_ids = feat_ref[0] * rows + pl.program_id(0) * bs + lax.broadcasted_iota(jnp.int32, (bs, PANEL), 0)
    hit = row_ids == lax.broadcasted_iota(jnp.int32, (bs, PANEL), 1)
    sh, sl = split2(s_ref[...] + jnp.where(hit, ridge_ref[0], 0.0))
    for b in range(PANEL // 256):
        r0, r1 = 256 * b, 256 * b + 256
        out = lax.dot_general(sh[:, :r1], low_ref[r0:r1, :r1], NT, preferred_element_type=jnp.float32)
        out += lax.dot_general(sl[:, :r1], high_ref[r0:r1, :r1], NT, preferred_element_type=jnp.float32)
        o_ref[:, r0:r1] = out + lax.dot_general(sh[:, :r1], high_ref[r0:r1, :r1], NT, preferred_element_type=jnp.float32)


def solve(feat, ridge, s, high, low, bs=384):
    rows = s.shape[0]
    smem = pl.BlockSpec(memory_space=pltpu.SMEM)
    return pl.pallas_call(
        functools.partial(solve_kernel, rows=rows),
        grid=(rows // bs,),
        out_shape=jax.ShapeDtypeStruct(s.shape, jnp.float32),
        in_specs=[smem, smem, pl.BlockSpec((bs, PANEL), lambda i: (i, 0)), *[pl.BlockSpec(memory_space=pltpu.VMEM)] * 2],
        out_specs=pl.BlockSpec((bs, PANEL), lambda i: (i, 0)),
        cost_estimate=pl.CostEstimate(flops=6 * rows * PANEL * PANEL, bytes_accessed=4 << 20, transcendentals=0),
        compiler_params=pltpu.CompilerParams(vmem_limit_bytes=65_600_000),
        name="solve",
    )(feat, ridge, s, high, low)


def feat_of(y, x, c):
    return ((y % SIDE) * SIDE + x % SIDE) * 2 + c


def permute(value, pairs):
    return lax.ppermute(value, "feat", pairs)


def share_panel(weights, earlier, tail, y, x, c):
    side = range(SIDE)
    root = (feat_of(0, 0, 0), feat_of(0, 0, 1))
    other = permute(earlier[:PANEL, PANEL:3 * PANEL], [root])

    def first_half(k):
        return weights[256 * k:256 * k + 256] if k < 2 else earlier[256 * (k - 2):256 * (k - 1), :PANEL]

    def last_half(k):
        return other[256 * (k % 2):256 * (k % 2) + 256, PANEL * (k // 2):PANEL * (k // 2) + PANEL]

    half = [jnp.where(c == 0, first_half(k), last_half(k)) for k in side]
    front = lax.optimization_barrier(jnp.concatenate([half[0], tail]))
    got = [permute(half[k], [(root[0], feat_of(0, k, 0)), (root[1], feat_of(k, 0, 1))]) for k in (2, 1, 3)]
    received = jnp.pad(got[0] + got[1] + got[2], ((0, EXTRA), (0, 0)))
    held = jnp.where((x == 0) & (y == 0), front, received)
    got = [
        permute(
            held,
            [(feat_of(0, j, 0), feat_of(k, j, 0)) for j in side] + [(feat_of(j, 0, 1), feat_of(j, k, 1)) for j in side],
        )
        for k in (2, 1, 3)
    ]
    held = jnp.where(jnp.where(c == 0, y, x) == 0, held, got[0] + got[1] + got[2])
    got = {
        k: permute(
            held,
            [(feat_of(i, j, 0), feat_of(i, j + k, 0)) for i in side for j in side]
            + [(feat_of(i, j, 1), feat_of(i + k, j, 1)) for i in side for j in side],
        )
        for k in (2, 1, 3)
    }
    own = [held, got[1], got[2], got[3]]
    partner = [permute(own[k], [(i, i ^ 1) for i in range(2 * SIDE * SIDE)]) for k in side]
    return own + partner


def on_device(data, omega, phase, earlier, ridge):
    samp, planes = lax.axis_size("samp"), lax.axis_size("feat")
    scale = math.sqrt(2.0 / (data.shape[0] * samp))
    feat = lax.axis_index("feat")
    y, x, c = place_of(feat)
    feat = feat.reshape(1)

    weights = omega.T
    turns = phase * INV_TURN
    first = lax.reduce_precision(turns, 8, 7)
    second = lax.reduce_precision(turns - first, 8, 7)
    third = turns - first - second
    tail = jnp.stack([first[:PANEL], second[:PANEL], third[:PANEL]]).astype(jnp.bfloat16)
    tail = jnp.concatenate([tail, jnp.zeros((EXTRA - 3, PANEL), jnp.bfloat16)])
    slots = share_panel(weights, earlier, tail, y, x, c)

    local = None
    blocks = data.shape[0] // SAMPLE_BLOCK
    edges = (0, blocks // 4, 5 * blocks // 8, blocks)
    for part in range(3):
        count = edges[part + 1] - edges[part]
        local = local_features(weights, turns[None], data, scale, edges[part], count, SAMPLE_BLOCK, local)
    s, d = gram(feat, slots, *[pltpu.with_memory_space_constraint(v, pltpu.HBM) for v in (data, local, earlier)], scale, samp)
    summed = lax.psum(s, "samp")
    d = lax.all_to_all(d, "samp", 0, 0).sum(0)
    d = lax.all_to_all(jnp.broadcast_to(d, (planes, 16, PANEL)), "feat", 0, 0)
    high, low = factor_inverse(ridge, d)
    return solve(feat, ridge, summed, high, low)


def solution(mesh):
    in_specs = (P("samp", None), P(None, "feat"), P("feat"), P("feat", "samp"), P())
    out_specs = P("feat", None)
    return jax.shard_map(on_device, mesh=mesh, in_specs=in_specs, out_specs=out_specs, check_vma=False)
```

```python
import functools
import math

import jax
import jax.numpy as jnp
import numpy as np
from jax import lax
from jax.experimental import pallas as pl
from jax.experimental.pallas import tpu as pltpu
from jax.sharding import PartitionSpec as P


PANEL = 512
SIDE = 4
SAMPLE_BLOCK = 512
EXTRA = 16
HIGHEST = lax.Precision.HIGHEST
NT = (((1,), (1,)), ((), ()))
TN = (((0,), (0,)), ((), ()))
INV_TURN = 1.0 / (2.0 * math.pi)
DEGREE = 3


def sine_coefficients():
    u = np.cos(np.pi * (np.arange(4000) + 0.5) / 4000) * 0.25
    fit = np.polynomial.chebyshev.Chebyshev.fit(u * u, -np.sin(2 * np.pi * u) / u, DEGREE, domain=[0, 1 / 16])
    poly = fit.convert(kind=np.polynomial.Polynomial, domain=[-1, 1], window=[-1, 1])
    return [float(v) for v in poly.coef]


SINE = sine_coefficients()


def scaled_cos(turns, scale):
    r = turns - jnp.round(turns)
    u = jnp.abs(r) - 0.25
    s = u * u
    coefs = [v * scale for v in SINE]
    p = coefs[DEGREE]
    for v in coefs[DEGREE - 1::-1]:
        p = p * s + v
    return p * u


def column(line):
    n = line.shape[1]
    eye = lax.broadcasted_iota(jnp.int32, (128, 128), 0) == lax.broadcasted_iota(jnp.int32, (128, 128), 1)
    parts = []
    for q in range(n // 128):
        square = jnp.broadcast_to(line[:, 128 * q:128 * q + 128], (128, 128))
        parts.append(jnp.sum(jnp.where(eye, square, 0.0), axis=1, keepdims=True))
    return jnp.concatenate(parts, axis=0)


def local_kernel(w_ref, ph_ref, x_ref, *refs, scale):
    o_ref, col_ref = refs[-2:]

    @pl.when(pl.program_id(0) == 0)
    def _():
        col_ref[...] = column(ph_ref[...])

    for r in range(w_ref.shape[0] // 256):
        part = slice(256 * r, 256 * r + 256)
        proj = lax.dot_general(w_ref[part, :], x_ref[...], NT, preferred_element_type=jnp.float32)
        o_ref[part, :] = scaled_cos(proj * INV_TURN + col_ref[part, :], scale).astype(jnp.bfloat16)


def local_features(wt, turns, data, scale, first, blocks, bs, before=None):
    rows, din = wt.shape
    samples = data.shape[0]
    done = [] if before is None else [before]
    return pl.pallas_call(
        functools.partial(local_kernel, scale=scale),
        grid=(blocks,),
        in_specs=[
            pl.BlockSpec((rows, din), lambda i: (0, 0)),
            pl.BlockSpec((1, rows), lambda i: (0, 0)),
            pl.BlockSpec((bs, din), lambda i: (first + i, 0)),
            *[pl.BlockSpec(memory_space=pl.ANY) for _ in done],
        ],
        out_specs=pl.BlockSpec((rows, bs), lambda i: (0, first + i)),
        out_shape=jax.ShapeDtypeStruct((rows, samples), jnp.bfloat16),
        scratch_shapes=[pltpu.VMEM((rows, 1), jnp.float32)],
        input_output_aliases={3: 0} if done else {},
        cost_estimate=pl.CostEstimate(flops=2 * rows * blocks * bs * din, bytes_accessed=3 * blocks * bs * din, transcendentals=0),
        name="local_features",
    )(wt, turns, data, *done)


def place_of(feat):
    return lax.div(feat, 2 * SIDE), lax.rem(lax.div(feat, 2), SIDE), lax.rem(feat, 2)


def gram_kernel(feat_ref, *refs, scale, sub):
    slots, (x_ref, f_ref, e_ref, s_ref, d_ref, v_ref, acc_ref, ph_ref, panel_ref) = refs[:8], refs[8:]
    i = pl.program_id(0)
    rows = s_ref.shape[0]
    y, x, c = place_of(feat_ref[0])
    first = pl.multiple_of(feat_ref[0] * 16, 16)

    def sixteen(p):
        within = pl.ds(pl.multiple_of(lax.rem(first, 256), 16), 16)
        return v_ref[p + lax.div(first, 256), within, :]

    def add(cols, left, right, negate=False):
        out = lax.dot_general(left, right, NT, preferred_element_type=jnp.float32)
        if negate:
            s_ref[:, cols] -= out[:rows]
            acc_ref[:, cols] -= out[rows:]
        else:
            s_ref[:, cols] += out[:rows]
            acc_ref[:, cols] += out[rows:]

    @pl.when(i == 0)
    def _():
        for k in range(SIDE):
            along_x = lax.rem(x - k + SIDE, SIDE)
            along_y = SIDE + lax.rem(y - k + SIDE, SIDE)
            v_ref[jnp.where(c == 0, along_x, along_y)] = slots[k][...]
            v_ref[jnp.where(c == 0, along_y, along_x)] = slots[SIDE + k][...]
        tail = v_ref[0, 256:256 + EXTRA, :].astype(jnp.float32)
        ph_ref[...] = column((tail[0:1] + tail[1:2]) + tail[2:3])
        s_ref[...] = jnp.zeros_like(s_ref)
        acc_ref[...] = jnp.zeros_like(acc_ref)

    for chunk in range(3):
        @pl.when(i == chunk)
        def _(chunk=chunk):
            left = jnp.concatenate([e_ref[...], sixteen(2 + 2 * chunk)], axis=0)
            for h in range(2):
                add(slice(256 * h, 256 * h + 256), left, v_ref[2 + 2 * chunk + h, :256, :], negate=True)

    for j in range(x_ref.shape[0] // sub):
        at = slice(j * sub, j * sub + sub)
        for h in range(2):
            half = slice(256 * h, 256 * h + 256)
            proj = lax.dot_general(v_ref[h, :256, :], x_ref[at, :], NT, preferred_element_type=jnp.float32)
            panel_ref[j, half, :] = scaled_cos(proj * INV_TURN + ph_ref[half, :], scale).astype(jnp.bfloat16)
    for j in range(x_ref.shape[0] // sub):
        at = slice(j * sub, j * sub + sub)
        mine = panel_ref[j, pl.ds(first, 16), :]
        left = jnp.concatenate([f_ref[:, at], mine], axis=0)
        for h in range(2):
            half = slice(256 * h, 256 * h + 256)
            add(half, left, panel_ref[j, half, :])

    @pl.when(i == pl.num_programs(0) - 1)
    def _():
        for k in range(d_ref.shape[0]):
            d_ref[k] = acc_ref[...]


def gram(feat, slots, data, local, earlier, scale, copies, bs=1024, sub=512):
    rows = earlier.shape[0]
    samples, din = data.shape
    return pl.pallas_call(
        functools.partial(gram_kernel, scale=scale, sub=sub),
        grid=(samples // bs,),
        in_specs=[
            pl.BlockSpec(memory_space=pltpu.SMEM),
            *[pl.BlockSpec(memory_space=pltpu.VMEM) for _ in slots],
            pl.BlockSpec((bs, din), lambda i: (i, 0)),
            pl.BlockSpec((rows, bs), lambda i: (0, i)),
            pl.BlockSpec((rows, PANEL), lambda i: (0, jnp.minimum(i, 2))),
        ],
        out_specs=[
            pl.BlockSpec((rows, PANEL), lambda i: (0, 0)),
            pl.BlockSpec((copies, 16, PANEL), lambda i: (0, 0, 0)),
        ],
        out_shape=[
            jax.ShapeDtypeStruct((rows, PANEL), jnp.float32),
            jax.ShapeDtypeStruct((copies, 16, PANEL), jnp.float32),
        ],
        scratch_shapes=[
            pltpu.VMEM((2 * SIDE, *slots[0].shape), jnp.bfloat16),
            pltpu.VMEM((16, PANEL), jnp.float32),
            pltpu.VMEM((PANEL, 1), jnp.float32),
            pltpu.VMEM((bs // sub, PANEL, sub), jnp.bfloat16),
        ],
        cost_estimate=pl.CostEstimate(flops=8 << 30, bytes_accessed=16 << 20, transcendentals=0),
        compiler_params=pltpu.CompilerParams(vmem_limit_bytes=50 << 20),
        name="gram",
    )(feat, *slots, data, local, earlier)


def split2(v):
    high = v.astype(jnp.bfloat16)
    return high, (v - high.astype(jnp.float32)).astype(jnp.bfloat16)


def split3(v):
    high = v.astype(jnp.bfloat16)
    rest = v - high.astype(jnp.float32)
    mid = rest.astype(jnp.bfloat16)
    return high, mid, (rest - mid.astype(jnp.float32)).astype(jnp.bfloat16)


def spread(block, j):
    return jnp.broadcast_to(block[:, j:j + 1], (8, 128))


def block_inverse(n_ref, lb_ref):
    sub = lax.broadcasted_iota(jnp.int32, (8, 128), 0)
    lane = lax.broadcasted_iota(jnp.int32, (8, 128), 1)

    def step(s, carry):
        rows0, rows1, left, right = carry
        k = pl.multiple_of(s * 8, 8)
        shift = jnp.where(s == 0, 0, 128 - k)
        n_ref[...] -= lax.dot_general(left, right, TN, preferred_element_type=jnp.float32)
        pivot = pltpu.roll(rows0, shift, 1)
        a = [[None] * 8 for _ in range(8)]
        for j in range(8):
            col = spread(pivot, j)
            for i in range(j, 8):
                a[i][j] = jnp.broadcast_to(col[i:i + 1, :], (8, 128))
        low = [[None] * 8 for _ in range(8)]
        root = []
        for j in range(8):
            inverse = 1.0 / a[j][j]
            root.append(lax.rsqrt(a[j][j]))
            for i in range(j + 1, 8):
                low[i][j] = a[i][j] * inverse
            for i in range(j + 1, 8):
                for m in range(j + 1, i + 1):
                    a[i][m] = a[i][m] - low[i][j] * a[m][j]
        t = [[None] * 8 for _ in range(8)]
        for j in range(8):
            t[j][j] = root[j]
            for i in range(j + 1, 8):
                acc = low[i][j]
                for m in range(j + 1, i):
                    acc = acc + low[i][m] * t[m][j]
                t[i][j] = -acc
        for j in range(8):
            for i in range(j + 1, 8):
                t[i][j] = root[i] * t[i][j]
        w0 = jnp.zeros((8, 128), jnp.float32)
        w1 = jnp.zeros((8, 128), jnp.float32)
        for j in range(8):
            col = jnp.where(sub == j, t[j][j], 0.0)
            for i in range(j + 1, 8):
                col = jnp.where(sub == i, t[i][j], col)
            w0 = w0 + col * jnp.broadcast_to(rows0[j:j + 1, :], (8, 128))
            w1 = w1 + col * jnp.broadcast_to(rows1[j:j + 1, :], (8, 128))
        lb_ref[pl.ds(k, 8), :] = w1
        after = jnp.minimum(k + 8, 120)
        after = pl.multiple_of(after, 8)
        next0 = n_ref[pl.ds(after, 8), :128]
        next1 = n_ref[pl.ds(after, 8), 128:]
        cross = pltpu.roll(next0, shift, 1)
        cols = [spread(cross, m) for m in range(8)]
        for j in range(8):
            factor = t[j][0] * cols[0]
            for m in range(1, j + 1):
                factor = factor + t[j][m] * cols[m]
            next0 = next0 - factor * jnp.broadcast_to(w0[j:j + 1, :], (8, 128))
            next1 = next1 - factor * jnp.broadcast_to(w1[j:j + 1, :], (8, 128))
        gh, gm, gl = split3(jnp.where(lane >= k + 8, w0, 0.0))
        wh, wm, wl = split3(jnp.concatenate([w0, w1], axis=1))
        left = jnp.concatenate([gh, gh, gm, gh, gm, gl], axis=0)
        right = jnp.concatenate([wh, wm, wh, wl, wm, wh], axis=0)
        return next0, next1, left, right

    start = (
        n_ref[:8, :128],
        n_ref[:8, 128:],
        jnp.zeros((48, 128), jnp.bfloat16),
        jnp.zeros((48, 256), jnp.bfloat16),
    )
    lax.fori_loop(0, 16, step, start)


def factor_kernel(ridge_ref, d_ref, high_ref, low_ref, m_ref, j_ref, n_ref, lb_ref):
    n = PANEL
    eye = lax.broadcasted_iota(jnp.int32, (n, n), 0) == lax.broadcasted_iota(jnp.int32, (n, n), 1)
    m_ref[...] = d_ref[...].reshape(n, n) + jnp.where(eye, ridge_ref[0], 0.0)
    j_ref[...] = jnp.where(eye, 1.0, 0.0)
    high_ref[...] = jnp.zeros((n, n), jnp.bfloat16)
    low_ref[...] = jnp.zeros((n, n), jnp.bfloat16)
    small = lax.broadcasted_iota(jnp.int32, (128, 128), 0) == lax.broadcasted_iota(jnp.int32, (128, 128), 1)
    for b in range(n // 128):
        r0, r1 = 128 * b, 128 * b + 128
        n_ref[:, :128] = m_ref[r0:r1, r0:r1]
        n_ref[:, 128:] = jnp.where(small, 1.0, 0.0)
        block_inverse(n_ref, lb_ref)
        lb = lb_ref[...]
        jb = jnp.dot(lb, j_ref[r0:r1, :r1], precision=HIGHEST, preferred_element_type=jnp.float32)
        high_ref[r0:r1, :r1], low_ref[r0:r1, :r1] = split2(jb)
        if r1 < n:
            r = jnp.dot(lb, m_ref[r0:r1, r1:], precision=HIGHEST, preferred_element_type=jnp.float32)
            m_ref[r1:, r1:] -= lax.dot_general(r, r, TN, precision=HIGHEST, preferred_element_type=jnp.float32)
            j_ref[r1:, :r1] -= lax.dot_general(r, jb, TN, precision=HIGHEST, preferred_element_type=jnp.float32)


def factor_inverse(ridge, d):
    n = PANEL
    return pl.pallas_call(
        factor_kernel,
        out_shape=[jax.ShapeDtypeStruct((n, n), jnp.bfloat16)] * 2,
        in_specs=[pl.BlockSpec(memory_space=pltpu.SMEM), pl.BlockSpec(memory_space=pltpu.VMEM)],
        out_specs=[pl.BlockSpec(memory_space=pltpu.VMEM)] * 2,
        scratch_shapes=[
            pltpu.VMEM((n, n), jnp.float32),
            pltpu.VMEM((n, n), jnp.float32),
            pltpu.VMEM((128, 256), jnp.float32),
            pltpu.VMEM((128, 128), jnp.float32),
        ],
        cost_estimate=pl.CostEstimate(flops=8 << 30, bytes_accessed=2 << 20, transcendentals=0),
        compiler_params=pltpu.CompilerParams(vmem_limit_bytes=12 << 20),
        name="factor_inverse",
    )(ridge, d)


def solve_kernel(feat_ref, ridge_ref, s_ref, high_ref, low_ref, o_ref, *, rows):
    bs = s_ref.shape[0]
    row_ids = feat_ref[0] * rows + pl.program_id(0) * bs + lax.broadcasted_iota(jnp.int32, (bs, PANEL), 0)
    hit = row_ids == lax.broadcasted_iota(jnp.int32, (bs, PANEL), 1)
    sh, sl = split2(s_ref[...] + jnp.where(hit, ridge_ref[0], 0.0))
    for b in range(PANEL // 256):
        r0, r1 = 256 * b, 256 * b + 256
        out = lax.dot_general(sh[:, :r1], low_ref[r0:r1, :r1], NT, preferred_element_type=jnp.float32)
        out += lax.dot_general(sl[:, :r1], high_ref[r0:r1, :r1], NT, preferred_element_type=jnp.float32)
        o_ref[:, r0:r1] = out + lax.dot_general(sh[:, :r1], high_ref[r0:r1, :r1], NT, preferred_element_type=jnp.float32)


def solve(feat, ridge, s, high, low, bs=384):
    rows = s.shape[0]
    smem = pl.BlockSpec(memory_space=pltpu.SMEM)
    return pl.pallas_call(
        functools.partial(solve_kernel, rows=rows),
        grid=(rows // bs,),
        out_shape=jax.ShapeDtypeStruct(s.shape, jnp.float32),
        in_specs=[smem, smem, pl.BlockSpec((bs, PANEL), lambda i: (i, 0)), *[pl.BlockSpec(memory_space=pltpu.VMEM)] * 2],
        out_specs=pl.BlockSpec((bs, PANEL), lambda i: (i, 0)),
        cost_estimate=pl.CostEstimate(flops=6 * rows * PANEL * PANEL, bytes_accessed=4 << 20, transcendentals=0),
        compiler_params=pltpu.CompilerParams(vmem_limit_bytes=65_600_000),
        name="solve",
    )(feat, ridge, s, high, low)


def feat_of(y, x, c):
    return ((y % SIDE) * SIDE + x % SIDE) * 2 + c


def permute(value, pairs):
    return lax.ppermute(value, "feat", pairs)


def share_panel(weights, earlier, tail, y, x, c):
    side = range(SIDE)
    root = (feat_of(0, 0, 0), feat_of(0, 0, 1))
    other = permute(earlier[:PANEL, PANEL:3 * PANEL], [root])

    def first_half(k):
        return weights[256 * k:256 * k + 256] if k < 2 else earlier[256 * (k - 2):256 * (k - 1), :PANEL]

    def last_half(k):
        return other[256 * (k % 2):256 * (k % 2) + 256, PANEL * (k // 2):PANEL * (k // 2) + PANEL]

    half = [jnp.where(c == 0, first_half(k), last_half(k)) for k in side]
    front = lax.optimization_barrier(jnp.concatenate([half[0], tail]))
    got = [permute(half[k], [(root[0], feat_of(0, k, 0)), (root[1], feat_of(k, 0, 1))]) for k in (1, 3, 2)]
    received = jnp.pad(got[0] + got[1] + got[2], ((0, EXTRA), (0, 0)))
    held = jnp.where((x == 0) & (y == 0), front, received)
    got = [
        permute(
            held,
            [(feat_of(0, j, 0), feat_of(k, j, 0)) for j in side] + [(feat_of(j, 0, 1), feat_of(j, k, 1)) for j in side],
        )
        for k in (1, 3, 2)
    ]
    held = jnp.where(jnp.where(c == 0, y, x) == 0, held, got[0] + got[1] + got[2])
    got = {
        k: permute(
            held,
            [(feat_of(i, j, 0), feat_of(i, j + k, 0)) for i in side for j in side]
            + [(feat_of(i, j, 1), feat_of(i + k, j, 1)) for i in side for j in side],
        )
        for k in (1, 3, 2)
    }
    own = [held, got[1], got[2], got[3]]
    partner = [permute(own[k], [(i, i ^ 1) for i in range(2 * SIDE * SIDE)]) for k in side]
    return own + partner


def on_device(data, omega, phase, earlier, ridge):
    samp, planes = lax.axis_size("samp"), lax.axis_size("feat")
    scale = math.sqrt(2.0 / (data.shape[0] * samp))
    feat = lax.axis_index("feat")
    y, x, c = place_of(feat)
    feat = feat.reshape(1)

    weights = omega.T
    turns = phase * INV_TURN
    first = lax.reduce_precision(turns, 8, 7)
    second = lax.reduce_precision(turns - first, 8, 7)
    third = turns - first - second
    tail = jnp.stack([first[:PANEL], second[:PANEL], third[:PANEL]]).astype(jnp.bfloat16)
    tail = jnp.concatenate([tail, jnp.zeros((EXTRA - 3, PANEL), jnp.bfloat16)])
    slots = share_panel(weights, earlier, tail, y, x, c)

    local = None
    blocks = data.shape[0] // SAMPLE_BLOCK
    edges = (0, blocks // 4, 5 * blocks // 8, blocks)
    for part in range(3):
        count = edges[part + 1] - edges[part]
        local = local_features(weights, turns[None], data, scale, edges[part], count, SAMPLE_BLOCK, local)
    s, d = gram(feat, slots, *[pltpu.with_memory_space_constraint(v, pltpu.HBM) for v in (data, local, earlier)], scale, samp)
    summed = lax.psum(s, "samp")
    d = lax.all_to_all(d, "samp", 0, 0).sum(0)
    d = lax.all_to_all(jnp.broadcast_to(d, (planes, 16, PANEL)), "feat", 0, 0)
    high, low = factor_inverse(ridge, d)
    return solve(feat, ridge, summed, high, low)


def solution(mesh):
    in_specs = (P("samp", None), P(None, "feat"), P("feat"), P("feat", "samp"), P())
    out_specs = P("feat", None)
    return jax.shard_map(on_device, mesh=mesh, in_specs=in_specs, out_specs=out_specs, check_vma=False)
```
